256 devices in a mesh: vol: 64 (over z, y, core), dsg: 4 (over x).
Axes of the slice: x: 4, y: 4, z: 8, core: 2. Of those that a mesh axis runs over, the one named last changes fastest.
Arguments:
- fields: float32 [262144, 128], P('vol'), may hold values from -6 to 6
- far_geom: float32 [8, 131072], P(None, ('vol', 'dsg')), may hold values from -6 to 6, as said below
- far_block: int32 [131072, 1], P(('vol', 'dsg')), may hold values from 0 to 63; in each aligned block of 512 rows (0 to 511, 512 to 1023, ...) at most 20 rows name the same one
- far_cell: int32 [131072], P(('vol', 'dsg')), may hold values from 0 to 4095
- far_patch: int32 [131072], P(('vol', 'dsg')), may hold values from 0 to 95, as said below
- near_geom: float32 [8, 524288], P(None, ('vol', 'dsg')), may hold values from -6 to 6, as said below
- near_cell: int32 [524288], P(('vol', 'dsg')), may hold values from 0 to 4095
- near_patch: int32 [524288], P(('vol', 'dsg')), may hold values from 0 to 95, as said below
- adjacency: int32 [96, 4], replicated, may hold values from -1 to 95, as said below
Outputs:
- far_density: float32 [131072], P(('vol', 'dsg'))
- design_grad: float32 [96, 64, 64], P('dsg')
The draws below stay inside these ranges and needn't reach their ends.
Inputs may be any that keep to these rules, and one draw needn't show every extreme that they name: `far_geom`: rows 0-2 and 6-7 lie in [0, 1). `near_geom`: rows 0-2 and 6-7 lie in [0, 1). `far_block`: the 512 far points of one device name each block at most 20 times. `far_patch`: the far and near points of one device lie on at most 4 design patches, the same set for both. `near_patch`: the far and near points of one device lie on at most 4 design patches, the same set for both. -1 marks a free side; where adjacency[k, s] = m >= 0, adjacency[m, s xor 1] = k.
All inputs are finite; a program needn't handle non-finite values.
Results may differ from the reference program's by a relative error of at most 0.0003.
Values sent between devices are 32-bit elements; how exact they have to be, the bound alone decides.
A program may use at most 128 MiB of HBM per device.

```python
import math
import jax
import jax.numpy as jnp
import numpy as np
from jax import lax

BASIS = 64
CELLS_DEV = 4096
PTS_DEV = 512
NEAR_DEV = 2048
CTRL = 64
CHORD_PATCHES = 12
SPAN_PATCHES = 8
PATCH_GRP = 4
SMOOTH_ITERS = 3
CAP = 20
CELLS = 262144
POINTS = 131072
NEAR = 524288
PATCHES = 96
N_VOL = 64
N_DSG = 4


def geometry(key, salt_value, point_total):
    base_key = jax.random.fold_in(key, salt_value)
    inside = jax.random.uniform(jax.random.fold_in(base_key, 1), (3, point_total), jnp.float32)
    normals = jnp.clip(1.5 * jax.random.normal(jax.random.fold_in(base_key, 2), (3, point_total), jnp.float32), -6.0, 6.0)
    surface = jax.random.uniform(jax.random.fold_in(base_key, 3), (2, point_total), jnp.float32)
    return jnp.concatenate([inside, normals, surface], 0)


def draw_far_geom(key, part):
    return geometry(key, 21, POINTS)


def draw_near_geom(key, part):
    return geometry(key, 22, NEAR)


def patch_choice(key, salt_value, per_device):
    device_keys = jax.random.split(jax.random.fold_in(key, 31), POINTS // PTS_DEV)
    groups = jax.vmap(lambda one_key: jax.random.permutation(one_key, PATCHES)[:PATCH_GRP])(device_keys)
    member = jax.random.randint(jax.random.fold_in(key, salt_value), (POINTS // PTS_DEV, per_device), 0, PATCH_GRP)
    return jnp.take_along_axis(groups.astype(jnp.int32), member, 1).reshape(-1).astype(jnp.int32)


def draw_far_patch(key, part):
    return patch_choice(key, 32, PTS_DEV)


def draw_near_patch(key, part):
    return patch_choice(key, 33, NEAR_DEV)


def draw_adjacency(key, part):
    placing = jax.random.permutation(jax.random.fold_in(key, 41), PATCHES).astype(jnp.int32)
    layout = placing.reshape(CHORD_PATCHES, SPAN_PATCHES)
    previous = jnp.roll(layout, 1, 0)
    following = jnp.roll(layout, -1, 0)
    free_side = jnp.full((CHORD_PATCHES, 1), -1, jnp.int32)
    lower_span = jnp.concatenate([free_side, layout[:, :-1]], 1)
    upper_span = jnp.concatenate([layout[:, 1:], free_side], 1)
    neighbour_ids = jnp.stack([previous, following, lower_span, upper_span], -1).reshape(PATCHES, 4)
    return jnp.zeros((PATCHES, 4), jnp.int32).at[placing].set(neighbour_ids)


def set_ends(result, key, low, top_value):
    extent = result.shape
    place = [jax.random.randint(jax.random.fold_in(key, axis), (), 0, extent[axis]) for axis in range(len(extent))]
    result = result.at[tuple(place)].set(low)
    longest = extent.index(max(extent))
    place[longest] = (place[longest] + 1) % extent[longest]
    return result.at[tuple(place)].set(top_value)


def levels(key, shape, pieces, smallest, high):
    def one(dim, shards_of):
        steps = jax.random.uniform(jax.random.fold_in(jax.random.fold_in(key, 6), dim), (shards_of,), jnp.float32, smallest / len(pieces), high / len(pieces))
        return jnp.repeat(jnp.exp(steps), shape[dim] // shards_of).reshape((-1,) + (1,) * (len(shape) - dim - 1))

    factor_of = one(*pieces[0])
    for cut in pieces[1:]:
        factor_of = factor_of * one(*cut)
    return factor_of


def shared_out(stream_key, own, number, rows, number_of, top, bound, skew):
    ranking = jax.random.permutation(stream_key, number_of)
    packed, common = portions_of(number_of, rows * top, bound, skew, True), portions_of(number_of, rows * top, bound, skew, False)
    places = jnp.arange(number_of)

    def named(tallies, offset_by):
        used = int((tallies > 0).sum())
        fixed = max(1, used // 4)
        moved = fixed + (places - fixed + offset_by * (used - fixed)) % max(1, number_of - fixed)
        return jnp.zeros((number_of,), jnp.int32).at[ranking[jnp.where(places < fixed, places, moved)]].set(jnp.asarray(tallies, jnp.int32))

    tallies = jnp.where(number % 4 == 0, named(packed, number // 4), named(common, number - number // 4 - 1))
    mixed = jax.random.permutation(jax.random.fold_in(own, 3), number_of)
    giver, receiver = mixed[0:number_of // 2 * 2:2], mixed[1:number_of // 2 * 2:2]
    margin = jnp.minimum(tallies[giver] - 1, bound - tallies[receiver]) // 2
    margin = jnp.where((giver == ranking[0]) | (receiver == ranking[0]) | (tallies[receiver] == 0), 0, jnp.maximum(margin, 0))
    moved = jax.random.randint(jax.random.fold_in(own, 4), (number_of // 2,), 0, 1 << 20) % (margin + 1)
    tallies = tallies.at[giver].add(-moved).at[receiver].add(moved)
    items = jnp.searchsorted(jnp.cumsum(tallies), jnp.arange(rows * top), side="right").astype(jnp.int32)
    table = items.reshape(top, rows).T
    table = table[jax.random.permutation(jax.random.fold_in(own, 1), rows)]
    offset_by = jax.random.randint(jax.random.fold_in(own, 2), (rows, 1), 0, top)
    return jnp.take_along_axis(table, (jnp.arange(top)[None, :] + offset_by) % top, axis=1)


def portions_of(number_of, total, limit, slope, full):
    weights = [(1 << 20) // math.isqrt(grade ** slope) + 1 for grade in range(1, number_of + 1)]
    largest = limit if full else min(limit, max(-(-total // number_of), total * weights[0] // sum(weights)))
    least = 1 if total - largest >= number_of - 1 else 0
    holding, rest = [largest] + [least] * (number_of - 1), total - largest - least * (number_of - 1)
    while rest > 0:
        free = [i for i in range(1, number_of) if holding[i] < largest] or [i for i in range(1, number_of) if holding[i] < limit]
        pool, remaining = sum([weights[i] for i in free]), rest
        for i in free:
            extra = min(limit - holding[i], max(1, remaining * weights[i] // pool), rest)
            holding[i] = holding[i] + extra
            rest = rest - extra
    return np.array(holding)


def gaussian(rng, extent, scale, most, cuts=(), held_as=jnp.bfloat16):
    drawn = scale * jax.random.normal(rng, extent, jnp.float32)
    if cuts:
        drawn = drawn * levels(rng, extent, cuts, -0.22, 0.18)
    return jnp.clip(drawn, -most, most).astype(held_as)


def setup_inputs(seed: int = 0) -> dict:
    key_of = jax.random.split(jax.random.key(seed), 10)
    fields = gaussian(key_of[0], (CELLS, 2 * BASIS), 1.0, 6.0, ((0, 64),), jnp.float32)
    far_geom = draw_far_geom(jax.random.fold_in(key_of[9], 71), 0)
    far_block_keys = jax.random.split(jax.random.fold_in(key_of[2], 1), POINTS // PTS_DEV)
    far_block_turns = jax.random.permutation(jax.random.fold_in(key_of[2], 3), POINTS // PTS_DEV)
    far_block = jax.vmap(lambda own, number: shared_out(jax.random.fold_in(key_of[2], 2), own, number, PTS_DEV, N_VOL, 1, CAP, 2))(far_block_keys, far_block_turns).reshape((POINTS, 1))
    far_cell = set_ends(jax.random.randint(key_of[3], (POINTS,), 0, CELLS_DEV), jax.random.fold_in(key_of[3], 1), 0, CELLS_DEV - 1).astype(jnp.int32)
    far_patch = draw_far_patch(jax.random.fold_in(key_of[9], 71), 0)
    near_geom = draw_near_geom(jax.random.fold_in(key_of[9], 71), 0)
    near_cell = set_ends(jax.random.randint(key_of[6], (NEAR,), 0, CELLS_DEV), jax.random.fold_in(key_of[6], 1), 0, CELLS_DEV - 1).astype(jnp.int32)
    near_patch = draw_near_patch(jax.random.fold_in(key_of[9], 71), 0)
    adjacency = draw_adjacency(jax.random.fold_in(key_of[9], 71), 0)
    return dict(fields=fields, far_geom=far_geom, far_block=far_block, far_cell=far_cell, far_patch=far_patch, near_geom=near_geom, near_cell=near_cell, near_patch=near_patch, adjacency=adjacency)


PENALTY = 4.0
SMOOTHING = 16.0
FLIPPED = np.array([1, 0, 3, 2], dtype=np.int32)

def bernstein(position):
    complement = 1.0 - position
    values = jnp.stack([complement * complement * complement, 3.0 * position * complement * complement, 3.0 * position * position * complement, position * position * position])
    slopes = jnp.stack([-3.0 * complement * complement, 3.0 * complement * complement - 6.0 * position * complement, 6.0 * position * complement - 3.0 * position * position, 3.0 * position * position])
    return (values, slopes)

def tensor_basis(factor_x, factor_y, factor_z):
    product = factor_x[:, None, None, :] * factor_y[None, :, None, :] * factor_z[None, None, :, :]
    return product.reshape(-1, factor_x.shape[-1])

def evaluate(columns, coords):
    value_x, slope_x = bernstein(coords[0])
    value_y, slope_y = bernstein(coords[1])
    value_z, slope_z = bernstein(coords[2])
    basis_set = [tensor_basis(value_x, value_y, value_z), tensor_basis(slope_x, value_y, value_z), tensor_basis(value_x, slope_y, value_z), tensor_basis(value_x, value_y, slope_z)]
    half_width = columns.shape[0] // 2
    state_part = columns[:half_width]
    adjoint_part = columns[half_width:]
    results = [jnp.sum(state_part * basis_kind, 0) for basis_kind in basis_set]
    results = results + [jnp.sum(adjoint_part * basis_kind, 0) for basis_kind in basis_set]
    return jnp.stack(results)

def density(values, normals):
    grad_state = values[1:4]
    grad_adjoint = values[5:8]
    normal_sq = jnp.sum(normals * normals, 0)
    inner_sum = jnp.sum(grad_state * grad_adjoint, 0)
    along_state = jnp.sum(grad_state * normals, 0)
    along_adjoint = jnp.sum(grad_adjoint * normals, 0)
    return normal_sq * inner_sum - 2.0 * along_state * along_adjoint + PENALTY * normal_sq * values[0] * values[4]

def spline_weights(param, span_count):
    scaled = param * span_count
    first_span = jnp.clip(jnp.floor(scaled), 0, span_count - 1)
    offset_in = scaled - first_span
    complement = 1.0 - offset_in
    cubed = offset_in * offset_in * offset_in
    squared = offset_in * offset_in
    weights = jnp.stack([complement * complement * complement / 6.0, (3.0 * cubed - 6.0 * squared + 4.0) / 6.0, (-3.0 * cubed + 3.0 * squared + 3.0 * offset_in + 1.0) / 6.0, cubed / 6.0])
    return (first_span.astype(jnp.int32), weights)

def spread(grid_flat, strength, spline_params, patch_ids, control):
    span_count = control - 3
    start_s, weights_s = spline_weights(spline_params[0], span_count)
    start_t, weights_t = spline_weights(spline_params[1], span_count)
    offsets = jnp.arange(4, dtype=jnp.int32)
    row_index = patch_ids[None, :] * control + start_s[None, :] + offsets[:, None]
    flat_index = (row_index[:, None, :] * control + start_t[None, None, :] + offsets[None, :, None]).reshape(-1)
    additions = (strength[None, None, :] * weights_s[:, None, :] * weights_t[None, :, :]).reshape(-1)
    return grid_flat.at[flat_index].add(additions)

def edge_table(iterate):
    return jnp.stack([iterate[:, 0, :], iterate[:, -1, :], iterate[:, :, 0], iterate[:, :, -1]], 1)

def lookup(edge_rows, neighbours):
    safe_ids = jnp.maximum(neighbours, 0)
    picked = edge_rows[safe_ids, FLIPPED[None, :]]
    return jnp.where((neighbours >= 0)[:, :, None], picked, jnp.zeros_like(picked))

def apply_operator(iterate, halo_rows):
    patch_count, edge_size = (iterate.shape[0], iterate.shape[1])
    padded = jnp.zeros((patch_count, edge_size + 2, edge_size + 2), iterate.dtype)
    padded = padded.at[:, 1:-1, 1:-1].set(iterate)
    padded = padded.at[:, 0, 1:-1].set(halo_rows[:, 0])
    padded = padded.at[:, -1, 1:-1].set(halo_rows[:, 1])
    padded = padded.at[:, 1:-1, 0].set(halo_rows[:, 2])
    padded = padded.at[:, 1:-1, -1].set(halo_rows[:, 3])
    beside = padded[:, :-2, 1:-1] + padded[:, 2:, 1:-1] + padded[:, 1:-1, :-2] + padded[:, 1:-1, 2:]
    return iterate + SMOOTHING * (4.0 * iterate - beside)

def precondition(residual):
    patch_count, edge_size = (residual.shape[0], residual.shape[1])
    below_diag = jnp.full((patch_count, edge_size), -SMOOTHING, residual.dtype).at[:, 0].set(0.0)
    main_diag = jnp.full((patch_count, edge_size), 1.0 + 2.0 * SMOOTHING, residual.dtype)
    above_diag = jnp.full((patch_count, edge_size), -SMOOTHING, residual.dtype).at[:, -1].set(0.0)
    along_rows = lax.linalg.tridiagonal_solve(below_diag, main_diag, above_diag, residual)
    along_cols = lax.linalg.tridiagonal_solve(below_diag, main_diag, above_diag, jnp.swapaxes(along_rows, 1, 2))
    return jnp.swapaxes(along_cols, 1, 2)

def smooth(summed, neighbours):
    iterate = precondition(summed)
    for sweep_index in range(SMOOTH_ITERS):
        halo_rows = lookup(edge_table(iterate), neighbours)
        iterate = iterate + precondition(summed - apply_operator(iterate, halo_rows))
    return iterate

def reference(fields, far_geom, far_block, far_cell, far_patch, near_geom, near_cell, near_patch, adjacency):
    columns_all = fields.T
    devices_count = POINTS // PTS_DEV
    grid_flat = jnp.zeros((PATCHES * CTRL * CTRL,), fields.dtype)
    far_cells = (far_block[:, 0] * CELLS_DEV + far_cell).astype(jnp.int32)
    owner_block = jnp.arange(devices_count, dtype=jnp.int32) // N_DSG * CELLS_DEV
    near_cells = (near_cell.reshape(devices_count, NEAR_DEV) + owner_block[:, None]).astype(jnp.int32)

    def point_step(carried, inputs):
        geom_part, cells_part, patch_part = inputs
        values = evaluate(jnp.take(columns_all, cells_part, axis=1), geom_part[0:3])
        strength = density(values, geom_part[3:6])
        return (spread(carried, strength, geom_part[6:8], patch_part, CTRL), strength)
    grid_flat, far_values = lax.scan(point_step, grid_flat, (far_geom.reshape(8, devices_count, PTS_DEV).transpose(1, 0, 2), far_cells.reshape(devices_count, PTS_DEV), far_patch.reshape(devices_count, PTS_DEV)))
    grid_flat, unused = lax.scan(point_step, grid_flat, (near_geom.reshape(8, devices_count, NEAR_DEV).transpose(1, 0, 2), near_cells, near_patch.reshape(devices_count, NEAR_DEV)))
    design = smooth(grid_flat.reshape(PATCHES, CTRL, CTRL), adjacency)
    return (far_values.reshape(-1), design)
```

```python
import jax
import jax.numpy as jnp
import numpy as np
from jax import lax
from jax.experimental import pallas as pl
from jax.experimental.pallas import tpu as pltpu
from jax.sharding import PartitionSpec as P

F32 = jnp.float32
BF16 = jnp.bfloat16
I32 = jnp.int32
MESH = pl.DeviceIdType.MESH

CTRL = 64
GROUP = 4
CAP = 20
PENALTY = 4.0
SMOOTHING = 16.0
LANES = 128
VOL = 64
DSG = 4
PATCHES = 96
OWN = PATCHES // DSG
HALF = OWN // 2
ROW = OWN * CTRL
NOBODY = 999.0


def constants():
    order = np.arange(1, CTRL + 1)
    sine = np.sqrt(2.0 / (CTRL + 1)) * np.sin(np.pi * np.outer(order, order) / (CTRL + 1))
    spectrum = 2.0 - 2.0 * np.cos(np.pi * order / (CTRL + 1))
    inverse = 1.0 / (1.0 + SMOOTHING * spectrum)
    power = [inverse * (1.0 - inverse) ** k for k in range(4)]
    ends = [sine[0], sine[-1]]
    zero = np.zeros((CTRL, CTRL))
    sine_pair = np.block([[sine, zero], [zero, sine]])
    total = sum(np.outer(p, p) for p in power)
    total_pair = np.concatenate([total, total], 1)

    def spread(k):
        scale = SMOOTHING * np.outer(power[k], power[k])
        table = np.zeros((4, CTRL, 4, CTRL))
        for side in range(4):
            for at in range(CTRL):
                unit = np.zeros(CTRL)
                unit[at] = 1.0
                end = ends[side % 2]
                field = scale * (np.outer(end, unit) if side < 2 else np.outer(unit, end))
                table[side, at, 0] = ends[0] @ field
                table[side, at, 1] = ends[1] @ field
                table[side, at, 2] = field @ ends[0]
                table[side, at, 3] = field @ ends[1]
        return table.reshape(4 * CTRL, 4 * CTRL)

    first = np.zeros((8, CTRL))
    lane_power = np.zeros((8, LANES))
    pair_first = np.zeros((16, LANES))
    pair_power = np.zeros((16, CTRL))
    for k in range(3):
        for side in range(2):
            row = 2 * k + side
            first[row] = power[k] * ends[side]
            lane_power[row] = np.tile(power[k], 2)
            for half in range(2):
                pair_first[6 * half + row, half * CTRL:(half + 1) * CTRL] = power[k] * ends[side]
                pair_power[6 * half + row] = power[k]
    tables = (sine, sine_pair, total_pair, spread(0), spread(1), first, lane_power, pair_first, pair_power)
    return [np.asarray(t, np.float32) for t in tables]


def iota(shape, axis):
    return lax.broadcasted_iota(I32, shape, axis)


def mm(a, b):
    return jnp.dot(a, b, preferred_element_type=F32)


def mm_nt(a, b):
    return lax.dot_general(a, b, (((1,), (1,)), ((), ())), preferred_element_type=F32)


def mm_tn(a, b):
    return lax.dot_general(a, b, (((0,), (0,)), ((), ())), preferred_element_type=F32)


def split2(x):
    high = x.astype(BF16)
    return high, (x - high.astype(F32)).astype(BF16)


def split3(x):
    high = x.astype(BF16)
    rest = x - high.astype(F32)
    middle = rest.astype(BF16)
    return high, middle, (rest - middle.astype(F32)).astype(BF16)


def exact(product, picks, x):
    high, middle, low = split3(x)
    picks = picks.astype(BF16)
    return product(picks, high) + product(picks, middle) + product(picks, low)


def dot3(product, a, b):
    a_high, a_low = split2(a)
    b_high, b_low = split2(b)
    return product(a_high, b_high) + product(a_high, b_low) + product(a_low, b_high)


def bernstein(t):
    c = 1.0 - t
    values = [c * c * c, 3.0 * t * c * c, 3.0 * t * t * c, t * t * t]
    slopes = [-3.0 * c * c, 3.0 * c * c - 6.0 * t * c, 6.0 * t * c - 3.0 * t * t, 3.0 * t * t]
    return values, slopes


def pick(index, rows):
    return jnp.where(
        index == 0, rows[0], jnp.where(index == 1, rows[1], jnp.where(index == 2, rows[2], rows[3]))
    )


def densities(columns, coords, normals):
    count = columns.shape[1]
    value_x, slope_x = bernstein(coords[0])
    value_y, slope_y = bernstein(coords[1])
    value_z, slope_z = bernstein(coords[2])
    place = iota((16, count), 0)
    at_y, at_z = place // 4, place % 4
    value_y, slope_y = pick(at_y, value_y), pick(at_y, slope_y)
    value_z, slope_z = pick(at_z, value_z), pick(at_z, slope_z)
    plain, with_y, with_z = value_y * value_z, slope_y * value_z, value_y * slope_z
    point = []
    for base in (0, 64):
        parts = [columns[base + 16 * i:base + 16 * i + 16] for i in range(4)]
        value = parts[0] * value_x[0] + parts[1] * value_x[1] + parts[2] * value_x[2] + parts[3] * value_x[3]
        slope = parts[0] * slope_x[0] + parts[1] * slope_x[1] + parts[2] * slope_x[2] + parts[3] * slope_x[3]
        products = (value * plain, slope * plain, value * with_y, value * with_z)
        point.append([jnp.sum(product, 0, keepdims=True) for product in products])
    (u, ux, uy, uz), (w, wx, wy, wz) = point
    nx, ny, nz = normals
    squared = nx * nx + ny * ny + nz * nz
    inner = ux * wx + uy * wy + uz * wz
    along_u = ux * nx + uy * ny + uz * nz
    along_w = wx * nx + wy * ny + wz * nz
    return squared * inner - 2.0 * along_u * along_w + PENALTY * squared * u * w


def spline(param):
    scaled = param * (CTRL - 3.0)
    start = jnp.clip(jnp.floor(scaled), 0.0, CTRL - 4.0)
    x = scaled - start
    c = 1.0 - x
    square, cube = x * x, x * x * x
    weights = (
        c * c * c / 6.0,
        (3.0 * cube - 6.0 * square + 4.0) / 6.0,
        (-3.0 * cube + 3.0 * square + 3.0 * x + 1.0) / 6.0,
        cube / 6.0,
    )
    offset = iota((CTRL, param.shape[1]), 0) - start.astype(I32)
    result = jnp.where(offset == 3, weights[3], 0.0)
    for k in (2, 1, 0):
        result = jnp.where(offset == k, weights[k], result)
    return result


def kernel(
    far_geom, block, far_cell, far_patch, near_geom, near_cell, near_patch, adjacency, fields,
    sine, sine_pair, total_pair, spread0, spread1, first, lane_power, pair_first, pair_power,
    far_out, design_out,
    rows, left, right, cells_v, cells_s, dens, ask, asked, reply, replied, grid, grids, part, parts,
    line, lines, edges, all_edges, halo, halo_rows, halo_cols,
    vol_send, vol_recv, dsg_send, dsg_recv, local_sem,
):
    me_vol = lax.axis_index("vol")
    me_dsg = lax.axis_index("dsg")
    far_count = far_geom.shape[1]
    near_count = near_geom.shape[1]

    barrier = pltpu.get_barrier_semaphore()

    def greet_vol(t, carry):
        peer = lax.rem(me_vol + t, VOL)
        pl.semaphore_signal(barrier, inc=1, device_id={"vol": peer}, device_id_type=MESH)
        return carry

    lax.fori_loop(1, VOL, greet_vol, 0)
    for t in range(1, DSG):
        peer = lax.rem(me_dsg + t, DSG)
        pl.semaphore_signal(barrier, inc=1, device_id={"dsg": peer}, device_id_type=MESH)

    def vol_copy(phase, source, target, t, at):
        peer = lax.rem(me_vol + t, VOL)
        return pltpu.make_async_remote_copy(
            src_ref=source(peer),
            dst_ref=target.at[at],
            send_sem=vol_send.at[phase, peer],
            recv_sem=vol_recv.at[phase, at],
            device_id={"vol": peer},
            device_id_type=MESH,
        )

    def vol_start(phase, source, target):
        def step(t, carry):
            vol_copy(phase, source, target, t, me_vol).start()
            return carry

        lax.fori_loop(1, VOL, step, 0)

    def vol_wait(phase, source, target):
        def step(t, carry):
            vol_copy(phase, source, target, t, lax.rem(me_vol + t, VOL)).wait()
            return carry

        lax.fori_loop(1, VOL, step, 0)

    def dsg_copy(phase, source, target, t, at):
        peer = lax.rem(me_dsg + t, DSG)
        return pltpu.make_async_remote_copy(
            src_ref=source(peer),
            dst_ref=target.at[at],
            send_sem=dsg_send.at[phase, peer],
            recv_sem=dsg_recv.at[phase, at],
            device_id={"dsg": peer},
            device_id_type=MESH,
        )

    def dsg_start(phase, source, target):
        for t in range(1, DSG):
            dsg_copy(phase, source, target, t, me_dsg).start()

    def dsg_wait(phase, source, target):
        for t in range(1, DSG):
            dsg_copy(phase, source, target, t, lax.rem(me_dsg + t, DSG)).wait()

    unseen = jnp.int32(PATCHES)
    near_ids, far_ids = near_patch[...], far_patch[...]
    ids = []
    previous = None
    for _ in range(GROUP):
        if previous is None:
            near_left, far_left = near_ids, far_ids
        else:
            near_left = jnp.where(near_ids > previous, near_ids, unseen)
            far_left = jnp.where(far_ids > previous, far_ids, unseen)
        previous = jnp.minimum(
            jnp.min(near_left, 1, keepdims=True), jnp.min(far_left, 1, keepdims=True)
        )
        ids.append(previous)

    to_block = iota((VOL, far_count), 0) == block[...]
    to_block_f = jnp.where(to_block, 1.0, 0.0)
    to_block_b = to_block_f.astype(BF16)
    earlier = jnp.where(
        iota((far_count, far_count), 0) < iota((far_count, far_count), 1), 1.0, 0.0
    ).astype(BF16)
    rank = jnp.sum(mm(to_block_b, earlier) * to_block_f, 0, keepdims=True).astype(I32)
    values = jnp.concatenate(
        [far_cell[...].astype(F32), far_geom[0:6, :], jnp.zeros((1, far_count), F32)], 0
    )
    placed = [jnp.where(rank == r, values, 0.0) for r in range(CAP)]
    placed.append(jnp.zeros((2 * LANES - 8 * CAP, far_count), F32))
    request = exact(mm_nt, to_block_b, jnp.concatenate(placed, 0))
    lane = iota((VOL, 2 * LANES), 1)
    for s in range(GROUP):
        request = jnp.where(lane == 8 * CAP + s, ids[s].astype(F32), request)
    ask[:, 0, :] = request
    asked[pl.ds(me_vol, 1)] = ask[pl.ds(me_vol, 1)]

    pl.semaphore_wait(barrier, VOL - 1 + DSG - 1)
    vol_start(0, lambda peer: ask.at[peer], asked)

    def take(cells, t, bounded=False):
        for r in range(LANES):
            cell = jnp.clip(cells[t, r], 0, fields.shape[0] - 1) if bounded else cells[t, r]
            rows[r:r + 1, :] = fields[pl.ds(cell, 1), :]
        return rows[...].T

    def scatter(at, strength, s_param, t_param, patch):
        left[:, pl.ds(at, LANES)] = spline(s_param)
        weights = spline(t_param) * strength
        for s in range(GROUP):
            right[s * CTRL:(s + 1) * CTRL, pl.ds(at, LANES)] = jnp.where(patch == ids[s], weights, 0.0)

    def near_chunk(t, carry):
        at = pl.multiple_of(t * LANES, LANES)
        columns = take(near_cell, t)
        geom = near_geom[:, pl.ds(at, LANES)]
        strength = densities(
            columns, [geom[i:i + 1] for i in range(3)], [geom[i:i + 1] for i in range(3, 6)]
        )
        scatter(at, strength, geom[6:7], geom[7:8], near_patch[:, pl.ds(at, LANES)])
        return carry

    chunks = near_count // LANES
    lax.fori_loop(0, chunks // 2, near_chunk, 0)

    vol_wait(0, lambda peer: ask.at[peer], asked)
    wanted = asked[:, 0, :].T
    tiles = []
    for t in range(CAP // 2):
        one = wanted[16 * t:16 * t + 8]
        two = wanted[16 * t + 8:16 * t + 16]
        tiles.append(jnp.concatenate([one, two], 1))
    cells_v[...] = jnp.concatenate(
        [jnp.clip((tile[0:1] + 0.5).astype(I32), 0, fields.shape[0] - 1) for tile in tiles] + [jnp.zeros((16 - CAP // 2, LANES), I32)], 0
    )
    to_scalar = pltpu.make_async_copy(cells_v, cells_s, local_sem)
    to_scalar.start()
    to_scalar.wait()
    dens[...] = jnp.zeros((LANES, LANES), F32)
    for t in range(CAP // 2):
        columns = take(cells_s, t, True)
        tile = tiles[t]
        strength = densities(
            columns, [tile[i:i + 1] for i in range(1, 4)], [tile[i:i + 1] for i in range(4, 7)]
        )
        dens[2 * t:2 * t + 1, 0:VOL] = strength[:, 0:VOL]
        dens[2 * t + 1:2 * t + 2, 0:VOL] = strength[:, VOL:]
    reply[:, 0, :] = dens[...].T[0:VOL, :]
    replied[pl.ds(me_vol, 1)] = reply[pl.ds(me_vol, 1)]
    vol_start(1, lambda peer: reply.at[peer], replied)

    lax.fori_loop(chunks // 2, chunks, near_chunk, 0)

    vol_wait(1, lambda peer: reply.at[peer], replied)
    answers = replied[:, 0, :].T
    high, middle, low = split3(answers)
    by_rank = mm(high, to_block_b) + mm(middle, to_block_b) + mm(low, to_block_b)
    far_strength = jnp.sum(
        jnp.where(iota((LANES, far_count), 0) == rank, by_rank, 0.0), 0, keepdims=True
    )
    far_out[...] = far_strength
    for t in range(far_count // LANES):
        at = slice(t * LANES, (t + 1) * LANES)
        scatter(
            near_count + t * LANES, far_strength[:, at], far_geom[6:7, at], far_geom[7:8, at], far_patch[:, at]
        )
    grid[:, 0, :] = dot3(mm_nt, left[...], right[...])
    grids[pl.ds(me_vol, 1)] = grid[pl.ds(me_vol, 1)]
    vol_start(2, lambda peer: grid.at[peer], grids)
    vol_wait(2, lambda peer: grid.at[peer], grids)

    got = grids[:, 0, :]
    patch_of = iota((PATCHES, VOL), 0).astype(F32)
    total = None
    for s in range(GROUP):
        place = jnp.where(patch_of == wanted[8 * CAP + s:8 * CAP + s + 1, :], 1.0, 0.0)
        term = exact(mm, place, got[:, s * CTRL:(s + 1) * CTRL])
        total = term if total is None else total + term
    total = dot3(mm, total, sine[...])
    for owner in range(DSG):
        base = owner * OWN
        pair = jnp.concatenate([total[base:base + HALF], total[base + HALF:base + OWN]], 1)
        for t in range(HALF):
            part[owner, :, t * LANES:(t + 1) * LANES] = pair[t:t + 1]
    parts[pl.ds(me_dsg, 1)] = part[pl.ds(me_dsg, 1)]
    dsg_start(0, lambda peer: part.at[peer], parts)
    dsg_wait(0, lambda peer: part.at[peer], parts)
    line[...] = parts[0] + parts[1] + parts[2] + parts[3]
    lines[pl.ds(me_vol, 1)] = line[...][None]
    vol_start(3, lambda peer: line, lines)
    vol_wait(3, lambda peer: line, lines)

    whole = dot3(mm, sine[...], lines[:, 0, :])
    span = [whole[:, t * LANES:(t + 1) * LANES] for t in range(HALF)]
    across = dot3(mm, first[...], whole)
    row_parts = [[], [], []]
    col_parts = [[], [], []]
    stacked = jnp.concatenate([across[:, t * LANES:(t + 1) * LANES] * lane_power[...] for t in range(HALF)], 0)
    edges_rows = stacked.reshape(HALF, 8, LANES)
    along = jnp.concatenate([dot3(mm_nt, pair_first[...], span[t]) * pair_power[...] for t in range(HALF)], 0)
    edges_cols = along.reshape(HALF, 16, CTRL)
    row_sum = [None, None]
    col_sum = [[None, None], [None, None]]
    for n in range(3):
        for side in range(2):
            term = edges_rows[:, 2 * n + side, :]
            row_sum[side] = term if n == 0 else row_sum[side] + term
            at = n * 4 * CTRL + side * CTRL
            edges[0:HALF, at:at + CTRL] = row_sum[side][:, 0:CTRL]
            edges[HALF:OWN, at:at + CTRL] = row_sum[side][:, CTRL:]
            for half in range(2):
                term = edges_cols[:, 6 * half + 2 * n + side, :]
                col_sum[half][side] = term if n == 0 else col_sum[half][side] + term
                at = n * 4 * CTRL + (2 + side) * CTRL
                edges[half * HALF:(half + 1) * HALF, at:at + CTRL] = col_sum[half][side]
    all_edges[pl.ds(me_dsg, 1)] = edges[...][None]
    dsg_start(1, lambda peer: edges, all_edges)
    dsg_wait(1, lambda peer: edges, all_edges)

    base = all_edges[...].reshape(PATCHES, 12 * CTRL)
    facing = [
        jnp.where(iota((PATCHES, PATCHES), 1) == adjacency[:, side:side + 1], 1.0, 0.0) for side in range(4)
    ]

    def exchange(edge):
        taken = []
        for side in range(4):
            other = side ^ 1
            taken.append(exact(mm, facing[side], edge[:, other * CTRL:(other + 1) * CTRL]))
        return jnp.concatenate(taken, 1)

    width = 4 * CTRL
    halo0 = exchange(base[:, 0:width])
    halo1 = exchange(base[:, width:2 * width] + dot3(mm, halo0, spread0[...]))
    halo2 = exchange(
        base[:, 2 * width:] + dot3(mm, halo0, spread1[...]) + dot3(mm, halo1, spread0[...])
    )
    halo[0], halo[1], halo[2] = halo0, halo1, halo2
    halo_rows[...] = jnp.zeros((HALF, 8, LANES), F32)
    halo_cols[...] = jnp.zeros((HALF, 16, CTRL), F32)
    mine = pl.ds(pl.multiple_of(me_dsg * OWN, 8), OWN)
    for k in range(3):
        own = halo[2 - k, mine, :]
        for side in range(2):
            row = 2 * k + side
            at = side * CTRL
            pair = jnp.concatenate([own[0:HALF, at:at + CTRL], own[HALF:OWN, at:at + CTRL]], 1)
            halo_rows[:, row, :] = pair * (SMOOTHING * lane_power[row:row + 1, :])
            at = (2 + side) * CTRL
            for half in range(2):
                halo_cols[:, 6 * half + row, :] = own[half * HALF:(half + 1) * HALF, at:at + CTRL] * (
                    SMOOTHING * pair_power[row:row + 1, :]
                )
    outcome = []
    for t in range(HALF):
        change = dot3(mm_tn, first[...], halo_rows[t]) + dot3(mm_tn, halo_cols[t], pair_first[...])
        outcome.append(span[t] * total_pair[...] + change)
    outcome = dot3(mm, jnp.concatenate(outcome, 0), sine_pair[...])
    for t in range(HALF):
        tile = dot3(mm, sine[...], outcome[t * CTRL:(t + 1) * CTRL])
        design_out[t] = tile[:, 0:CTRL]
        design_out[t + HALF] = tile[:, CTRL:]


def per_device(
    fields, far_geom, far_block, far_cell, far_patch, near_geom, near_cell, near_patch, adjacency
):
    far_count = far_cell.shape[0]
    near_count = near_cell.shape[0]
    points = far_count + near_count
    vmem = pl.BlockSpec(memory_space=pltpu.VMEM)
    smem = pl.BlockSpec(memory_space=pltpu.SMEM)
    tables = [jnp.asarray(t) for t in constants()]
    far, design = pl.pallas_call(
        kernel,
        out_shape=(
            jax.ShapeDtypeStruct((1, far_count), F32),
            jax.ShapeDtypeStruct((OWN, CTRL, CTRL), F32),
        ),
        in_specs=[vmem] * 5 + [smem] + [vmem] * (3 + len(tables)),
        out_specs=(vmem, vmem),
        scratch_shapes=[
            pltpu.VMEM((LANES, LANES), F32),
            pltpu.VMEM((CTRL, points), F32),
            pltpu.VMEM((GROUP * CTRL, points), F32),
            pltpu.VMEM((16, LANES), I32),
            pltpu.SMEM((16, LANES), I32),
            pltpu.VMEM((LANES, LANES), F32),
            pltpu.VMEM((VOL, 1, 2 * LANES), F32),
            pltpu.VMEM((VOL, 1, 2 * LANES), F32),
            pltpu.VMEM((VOL, 1, LANES), F32),
            pltpu.VMEM((VOL, 1, LANES), F32),
            pltpu.VMEM((VOL, 1, GROUP * CTRL), F32),
            pltpu.VMEM((VOL, 1, GROUP * CTRL), F32),
            pltpu.VMEM((DSG, 1, ROW), F32),
            pltpu.VMEM((DSG, 1, ROW), F32),
            pltpu.VMEM((1, ROW), F32),
            pltpu.VMEM((VOL, 1, ROW), F32),
            pltpu.VMEM((OWN, 12 * CTRL), F32),
            pltpu.VMEM((DSG, OWN, 12 * CTRL), F32),
            pltpu.VMEM((3, PATCHES, 4 * CTRL), F32),
            pltpu.VMEM((HALF, 8, LANES), F32),
            pltpu.VMEM((HALF, 16, CTRL), F32),
            pltpu.SemaphoreType.DMA((4, VOL)),
            pltpu.SemaphoreType.DMA((4, VOL)),
            pltpu.SemaphoreType.DMA((2, DSG)),
            pltpu.SemaphoreType.DMA((2, DSG)),
            pltpu.SemaphoreType.DMA,
        ],
        compiler_params=pltpu.CompilerParams(
            collective_id=0, has_side_effects=True, vmem_limit_bytes=60000 * 1024
        ),
    )(
        far_geom,
        far_block.reshape(1, far_count),
        far_cell.reshape(1, far_count),
        far_patch.reshape(1, far_count),
        near_geom,
        near_cell.reshape(near_count // LANES, LANES),
        near_patch.reshape(1, near_count),
        adjacency,
        fields,
        *tables,
    )
    return far.reshape(far_count), design


def solution(mesh):
    return jax.shard_map(
        per_device,
        mesh=mesh,
        in_specs=(
            P("vol", None),
            P(None, ("vol", "dsg")),
            P(("vol", "dsg"), None),
            P(("vol", "dsg")),
            P(("vol", "dsg")),
            P(None, ("vol", "dsg")),
            P(("vol", "dsg")),
            P(("vol", "dsg")),
            P(),
        ),
        out_specs=(P(("vol", "dsg")), P("dsg", None, None)),
        check_vma=False,
    )
```

```python
import jax
import jax.numpy as jnp
import numpy as np
from jax import lax
from jax.experimental import pallas as pl
from jax.experimental.pallas import tpu as pltpu
from jax.sharding import PartitionSpec as P

F32 = jnp.float32
BF16 = jnp.bfloat16
I32 = jnp.int32
MESH = pl.DeviceIdType.MESH

CTRL = 64
GROUP = 4
CAP = 20
PENALTY = 4.0
SMOOTHING = 16.0
LANES = 128
VOL = 64
VOL_Z = 8
VOL_Y = 4
VOL_C = 2
DSG = 4
PATCHES = 96
OWN = PATCHES // DSG
HALF = OWN // 2
ROW = OWN * CTRL
NOBODY = 999.0


def constants():
    order = np.arange(1, CTRL + 1)
    sine = np.sqrt(2.0 / (CTRL + 1)) * np.sin(np.pi * np.outer(order, order) / (CTRL + 1))
    spectrum = 2.0 - 2.0 * np.cos(np.pi * order / (CTRL + 1))
    inverse = 1.0 / (1.0 + SMOOTHING * spectrum)
    power = [inverse * (1.0 - inverse) ** k for k in range(4)]
    ends = [sine[0], sine[-1]]
    zero = np.zeros((CTRL, CTRL))
    sine_pair = np.block([[sine, zero], [zero, sine]])
    total = sum(np.outer(p, p) for p in power)
    total_pair = np.concatenate([total, total], 1)

    def spread(k):
        scale = SMOOTHING * np.outer(power[k], power[k])
        table = np.zeros((4, CTRL, 4, CTRL))
        for side in range(4):
            for at in range(CTRL):
                unit = np.zeros(CTRL)
                unit[at] = 1.0
                end = ends[side % 2]
                field = scale * (np.outer(end, unit) if side < 2 else np.outer(unit, end))
                table[side, at, 0] = ends[0] @ field
                table[side, at, 1] = ends[1] @ field
                table[side, at, 2] = field @ ends[0]
                table[side, at, 3] = field @ ends[1]
        return table.reshape(4 * CTRL, 4 * CTRL)

    first = np.zeros((8, CTRL))
    lane_power = np.zeros((8, LANES))
    pair_first = np.zeros((16, LANES))
    pair_power = np.zeros((16, CTRL))
    for k in range(3):
        for side in range(2):
            row = 2 * k + side
            first[row] = power[k] * ends[side]
            lane_power[row] = np.tile(power[k], 2)
            for half in range(2):
                pair_first[6 * half + row, half * CTRL:(half + 1) * CTRL] = power[k] * ends[side]
                pair_power[6 * half + row] = power[k]
    tables = (sine, sine_pair, total_pair, spread(0), spread(1), first, lane_power, pair_first, pair_power)
    return [np.asarray(t, np.float32) for t in tables]


def iota(shape, axis):
    return lax.broadcasted_iota(I32, shape, axis)


def mm(a, b):
    return jnp.dot(a, b, preferred_element_type=F32)


def mm_nt(a, b):
    return lax.dot_general(a, b, (((1,), (1,)), ((), ())), preferred_element_type=F32)


def mm_tn(a, b):
    return lax.dot_general(a, b, (((0,), (0,)), ((), ())), preferred_element_type=F32)


def split2(x):
    high = x.astype(BF16)
    return high, (x - high.astype(F32)).astype(BF16)


def split3(x):
    high = x.astype(BF16)
    rest = x - high.astype(F32)
    middle = rest.astype(BF16)
    return high, middle, (rest - middle.astype(F32)).astype(BF16)


def exact(product, picks, x):
    high, middle, low = split3(x)
    picks = picks.astype(BF16)
    return product(picks, high) + product(picks, middle) + product(picks, low)


def dot3(product, a, b):
    a_high, a_low = split2(a)
    b_high, b_low = split2(b)
    return product(a_high, b_high) + product(a_high, b_low) + product(a_low, b_high)


def bernstein(t):
    c = 1.0 - t
    values = [c * c * c, 3.0 * t * c * c, 3.0 * t * t * c, t * t * t]
    slopes = [-3.0 * c * c, 3.0 * c * c - 6.0 * t * c, 6.0 * t * c - 3.0 * t * t, 3.0 * t * t]
    return values, slopes


def pick(index, rows):
    return jnp.where(
        index == 0, rows[0], jnp.where(index == 1, rows[1], jnp.where(index == 2, rows[2], rows[3]))
    )


def densities(columns, coords, normals):
    count = columns.shape[1]
    value_x, slope_x = bernstein(coords[0])
    value_y, slope_y = bernstein(coords[1])
    value_z, slope_z = bernstein(coords[2])
    place = iota((16, count), 0)
    at_y, at_z = place // 4, place % 4
    value_y, slope_y = pick(at_y, value_y), pick(at_y, slope_y)
    value_z, slope_z = pick(at_z, value_z), pick(at_z, slope_z)
    plain, with_y, with_z = value_y * value_z, slope_y * value_z, value_y * slope_z
    point = []
    for base in (0, 64):
        parts = [columns[base + 16 * i:base + 16 * i + 16] for i in range(4)]
        value = parts[0] * value_x[0] + parts[1] * value_x[1] + parts[2] * value_x[2] + parts[3] * value_x[3]
        slope = parts[0] * slope_x[0] + parts[1] * slope_x[1] + parts[2] * slope_x[2] + parts[3] * slope_x[3]
        products = (value * plain, slope * plain, value * with_y, value * with_z)
        point.append([jnp.sum(product, 0, keepdims=True) for product in products])
    (u, ux, uy, uz), (w, wx, wy, wz) = point
    nx, ny, nz = normals
    squared = nx * nx + ny * ny + nz * nz
    inner = ux * wx + uy * wy + uz * wz
    along_u = ux * nx + uy * ny + uz * nz
    along_w = wx * nx + wy * ny + wz * nz
    return squared * inner - 2.0 * along_u * along_w + PENALTY * squared * u * w


def spline(param):
    scaled = param * (CTRL - 3.0)
    start = jnp.clip(jnp.floor(scaled), 0.0, CTRL - 4.0)
    x = scaled - start
    c = 1.0 - x
    square, cube = x * x, x * x * x
    weights = (
        c * c * c / 6.0,
        (3.0 * cube - 6.0 * square + 4.0) / 6.0,
        (-3.0 * cube + 3.0 * square + 3.0 * x + 1.0) / 6.0,
        cube / 6.0,
    )
    offset = iota((CTRL, param.shape[1]), 0) - start.astype(I32)
    result = jnp.where(offset == 3, weights[3], 0.0)
    for k in (2, 1, 0):
        result = jnp.where(offset == k, weights[k], result)
    return result


def kernel(
    far_geom, block, far_cell, far_patch, near_geom, near_cell, near_patch, adjacency,
    fields_in, sine_in, sine_pair_in, total_pair_in, spread0_in, spread1_in, first_in, lane_power_in,
    pair_first_in, pair_power_in,
    far_out, design_out,
    fields, sine, sine_pair, total_pair, spread0, spread1, first, lane_power, pair_first, pair_power,
    rows, left, right, cells_v, cells_s, dens, ask, asked, reply, replied, grid, grids, part, parts,
    line, lines, edges, all_edges, halo, halo_rows, halo_cols,
    vol_send, vol_recv, dsg_send, dsg_recv, z_send, z_recv, y_send, y_recv, core_send, core_recv,
    local_sem, load_sem, fields_sem,
):
    me_vol = lax.axis_index("vol")
    me_dsg = lax.axis_index("dsg")
    far_count = far_geom.shape[1]
    near_count = near_geom.shape[1]

    load_fields = pltpu.make_async_copy(fields_in, fields, fields_sem)
    load_fields.start()
    loads = [
        pltpu.make_async_copy(source, target, load_sem.at[i])
        for i, (source, target) in enumerate(
            (
                (sine_in, sine), (sine_pair_in, sine_pair), (total_pair_in, total_pair),
                (spread0_in, spread0), (spread1_in, spread1), (first_in, first),
                (lane_power_in, lane_power), (pair_first_in, pair_first), (pair_power_in, pair_power),
            )
        )
    ]
    for load in loads:
        load.start()

    barrier = pltpu.get_barrier_semaphore()

    def greet_vol(t, carry):
        peer = jnp.where(me_vol + t >= VOL, me_vol + t - VOL, me_vol + t)
        pl.semaphore_signal(barrier, inc=1, device_id={"vol": peer}, device_id_type=MESH)
        return carry

    lax.fori_loop(1, VOL, greet_vol, 0)
    for t in range(1, DSG):
        peer = jnp.where(me_dsg + t >= DSG, me_dsg + t - DSG, me_dsg + t)
        pl.semaphore_signal(barrier, inc=1, device_id={"dsg": peer}, device_id_type=MESH)

    def wrap(index, size):
        return jnp.where(index >= size, index - size, index)

    def vol_start(phase, source, target):
        def step(t, carry):
            peer = wrap(me_vol + t, VOL)
            pltpu.make_async_remote_copy(
                src_ref=source.at[peer],
                dst_ref=target.at[me_vol],
                send_sem=vol_send.at[phase],
                recv_sem=vol_recv.at[phase],
                device_id={"vol": peer},
                device_id_type=MESH,
            ).start()
            return carry

        lax.fori_loop(1, VOL, step, 0)

    def settle(ref, sem):
        pltpu.make_async_copy(ref, ref, sem).wait()

    def vol_wait(phase, source, target):
        settle(target.at[pl.ds(0, VOL - 1)], vol_recv.at[phase])
        settle(source.at[pl.ds(0, VOL - 1)], vol_send.at[phase])

    def dsg_start(phase, source, target):
        for t in range(1, DSG):
            peer = wrap(me_dsg + t, DSG)
            pltpu.make_async_remote_copy(
                src_ref=source(peer),
                dst_ref=target.at[me_dsg],
                send_sem=dsg_send.at[phase],
                recv_sem=dsg_recv.at[phase],
                device_id={"dsg": peer},
                device_id_type=MESH,
            ).start()

    def dsg_wait(phase, target):
        settle(target.at[pl.ds(0, DSG - 1)], dsg_recv.at[phase])
        settle(target.at[pl.ds(0, DSG - 1)], dsg_send.at[phase])

    unseen = jnp.int32(PATCHES)
    near_ids, far_ids = near_patch[...], far_patch[...]
    ids = []
    previous = None
    for _ in range(GROUP):
        if previous is None:
            near_left, far_left = near_ids, far_ids
        else:
            near_left = jnp.where(near_ids > previous, near_ids, unseen)
            far_left = jnp.where(far_ids > previous, far_ids, unseen)
        previous = jnp.minimum(
            jnp.min(near_left, 1, keepdims=True), jnp.min(far_left, 1, keepdims=True)
        )
        ids.append(previous)

    to_block = iota((VOL, far_count), 0) == block[...]
    to_block_f = jnp.where(to_block, 1.0, 0.0)
    to_block_b = to_block_f.astype(BF16)
    earlier = jnp.where(
        iota((far_count, far_count), 0) < iota((far_count, far_count), 1), 1.0, 0.0
    ).astype(BF16)
    rank = jnp.sum(mm(to_block_b, earlier) * to_block_f, 0, keepdims=True).astype(I32)
    values = jnp.concatenate(
        [far_cell[...].astype(F32), far_geom[0:6, :], jnp.zeros((1, far_count), F32)], 0
    )
    placed = [jnp.where(rank == r, values, 0.0) for r in range(CAP)]
    placed.append(jnp.zeros((2 * LANES - 8 * CAP, far_count), F32))
    request = exact(mm_nt, to_block_b, jnp.concatenate(placed, 0))
    lane = iota((VOL, 2 * LANES), 1)
    for s in range(GROUP):
        request = jnp.where(lane == 8 * CAP + s, ids[s].astype(F32), request)
    ask[:, 0, :] = request
    asked[pl.ds(me_vol, 1)] = ask[pl.ds(me_vol, 1)]

    sides = jnp.concatenate(
        [jnp.concatenate([adjacency[...], jnp.full((4, LANES - PATCHES), -1, I32)], 1)] * 2, 0
    ).astype(F32).T[0:PATCHES]
    patch_lane = iota((PATCHES, PATCHES), 1).astype(F32)
    facing = [jnp.where(patch_lane == sides[:, side:side + 1], 1.0, 0.0).astype(BF16) for side in range(4)]

    pl.semaphore_wait(barrier, VOL - 1 + DSG - 1)
    vol_start(0, ask, asked)

    def take(cells, t, bounded=False):
        for r in range(LANES):
            cell = jnp.clip(cells[t, r], 0, fields.shape[0] - 1) if bounded else cells[t, r]
            rows[r:r + 1, :] = fields[pl.ds(cell, 1), :]
        return rows[...].T

    def scatter(at, strength, s_param, t_param, patch):
        left[:, pl.ds(at, LANES)] = spline(s_param)
        weights = spline(t_param) * strength
        for s in range(GROUP):
            right[s * CTRL:(s + 1) * CTRL, pl.ds(at, LANES)] = jnp.where(patch == ids[s], weights, 0.0)

    def near_chunk(t, carry):
        at = pl.multiple_of(t * LANES, LANES)
        columns = take(near_cell, t)
        geom = near_geom[:, pl.ds(at, LANES)]
        strength = densities(
            columns, [geom[i:i + 1] for i in range(3)], [geom[i:i + 1] for i in range(3, 6)]
        )
        scatter(at, strength, geom[6:7], geom[7:8], near_patch[:, pl.ds(at, LANES)])
        return carry

    load_fields.wait()
    chunks = near_count // LANES
    lax.fori_loop(0, chunks // 2, near_chunk, 0)

    vol_wait(0, ask, asked)
    wanted = asked[:, 0, :].T
    tiles = []
    for t in range(CAP // 2):
        one = wanted[16 * t:16 * t + 8]
        two = wanted[16 * t + 8:16 * t + 16]
        tiles.append(jnp.concatenate([one, two], 1))
    cells_v[...] = jnp.concatenate(
        [jnp.clip((tile[0:1] + 0.5).astype(I32), 0, fields.shape[0] - 1) for tile in tiles] + [jnp.zeros((16 - CAP // 2, LANES), I32)], 0
    )
    to_scalar = pltpu.make_async_copy(cells_v, cells_s, local_sem)
    to_scalar.start()
    to_scalar.wait()
    dens[...] = jnp.zeros((LANES, LANES), F32)
    for t in range(CAP // 2):
        columns = take(cells_s, t, True)
        tile = tiles[t]
        strength = densities(
            columns, [tile[i:i + 1] for i in range(1, 4)], [tile[i:i + 1] for i in range(4, 7)]
        )
        dens[2 * t:2 * t + 1, 0:VOL] = strength[:, 0:VOL]
        dens[2 * t + 1:2 * t + 2, 0:VOL] = strength[:, VOL:]
    reply[:, 0, :] = dens[...].T[0:VOL, :]
    replied[pl.ds(me_vol, 1)] = reply[pl.ds(me_vol, 1)]
    vol_start(1, reply, replied)

    lax.fori_loop(chunks // 2, chunks, near_chunk, 0)

    vol_wait(1, reply, replied)
    answers = replied[:, 0, :].T
    high, middle, low = split3(answers)
    by_rank = mm(high, to_block_b) + mm(middle, to_block_b) + mm(low, to_block_b)
    far_strength = jnp.sum(
        jnp.where(iota((LANES, far_count), 0) == rank, by_rank, 0.0), 0, keepdims=True
    )
    far_out[...] = far_strength
    for t in range(far_count // LANES):
        at = slice(t * LANES, (t + 1) * LANES)
        scatter(
            near_count + t * LANES, far_strength[:, at], far_geom[6:7, at], far_geom[7:8, at], far_patch[:, at]
        )
    grid[:, 0, :] = dot3(mm_nt, left[...], right[...])
    grids[pl.ds(me_vol, 1)] = grid[pl.ds(me_vol, 1)]
    vol_start(2, grid, grids)
    vol_wait(2, grid, grids)

    got = grids[:, 0, :]
    patch_of = iota((PATCHES, VOL), 0).astype(F32)
    total = None
    for s in range(GROUP):
        place = jnp.where(patch_of == wanted[8 * CAP + s:8 * CAP + s + 1, :], 1.0, 0.0)
        term = exact(mm, place, got[:, s * CTRL:(s + 1) * CTRL])
        total = term if total is None else total + term
    loads[0].wait()
    total = dot3(mm, total, sine[...])
    for owner in range(DSG):
        base = owner * OWN
        pair = jnp.concatenate([total[base:base + HALF], total[base + HALF:base + OWN]], 1)
        for t in range(HALF):
            part[owner, :, t * LANES:(t + 1) * LANES] = pair[t:t + 1]
    parts[pl.ds(me_dsg, 1)] = part[pl.ds(me_dsg, 1)]
    dsg_start(0, lambda peer: part.at[peer], parts)
    dsg_wait(0, parts)
    line[...] = parts[0] + parts[1] + parts[2] + parts[3]
    me_z, me_y, me_c = me_vol // (VOL_Y * VOL_C), me_vol // VOL_C % VOL_Y, me_vol % VOL_C

    def at_vol(z, y, c):
        return (z * VOL_Y + y) * VOL_C + c

    lines[me_z, me_y, me_c] = line[...]
    ring = (1, 7, 2, 6, 3, 5, 4)
    for turn in ring:
        pltpu.make_async_remote_copy(
            src_ref=line,
            dst_ref=lines.at[me_z, me_y, me_c],
            send_sem=z_send,
            recv_sem=z_recv.at[turn],
            device_id={"vol": at_vol(wrap(me_z + turn, VOL_Z), me_y, me_c)},
            device_id_type=MESH,
        ).start()

    def to_core(source, target):
        pltpu.make_async_remote_copy(
            src_ref=source,
            dst_ref=target,
            send_sem=core_send,
            recv_sem=core_recv,
            device_id={"vol": at_vol(me_z, me_y, 1 - me_c)},
            device_id_type=MESH,
        ).start()

    for turn in (0,) + ring:
        z = wrap(me_z + VOL_Z - turn, VOL_Z)
        target = lines.at[z, me_y, me_c]
        source = line if turn == 0 else target
        if turn:
            settle(target, z_recv.at[turn])
        for step in (2, 1, 3):
            pltpu.make_async_remote_copy(
                src_ref=source,
                dst_ref=target,
                send_sem=y_send,
                recv_sem=y_recv.at[step],
                device_id={"vol": at_vol(me_z, wrap(me_y + step, VOL_Y), me_c)},
                device_id_type=MESH,
            ).start()
        to_core(source, target)
    for step in (1, 3, 2):
        y = wrap(me_y + VOL_Y - step, VOL_Y)
        column = lines.at[:, y, me_c]
        settle(column, y_recv.at[step])
        to_core(column, column)
    settle(lines.at[:, :, 0], core_recv)
    settle(lines.at[pl.ds(0, VOL_Z - 1), 0, 0], z_send)
    settle(lines.at[:, pl.ds(0, VOL_Y - 1), 0], y_send)
    settle(lines.at[:, :, 0], core_send)

    for load in loads[1:]:
        load.wait()
    whole = dot3(mm, sine[...], lines[...].reshape(VOL, ROW))
    span = [whole[:, t * LANES:(t + 1) * LANES] for t in range(HALF)]
    across = dot3(mm, first[...], whole)
    row_parts = [[], [], []]
    col_parts = [[], [], []]
    stacked = jnp.concatenate([across[:, t * LANES:(t + 1) * LANES] * lane_power[...] for t in range(HALF)], 0)
    edges_rows = stacked.reshape(HALF, 8, LANES)
    along = jnp.concatenate([dot3(mm_nt, pair_first[...], span[t]) * pair_power[...] for t in range(HALF)], 0)
    edges_cols = along.reshape(HALF, 16, CTRL)
    row_sum = [None, None]
    col_sum = [[None, None], [None, None]]
    for n in range(3):
        for side in range(2):
            term = edges_rows[:, 2 * n + side, :]
            row_sum[side] = term if n == 0 else row_sum[side] + term
            at = n * 4 * CTRL + side * CTRL
            edges[0:HALF, at:at + CTRL] = row_sum[side][:, 0:CTRL]
            edges[HALF:OWN, at:at + CTRL] = row_sum[side][:, CTRL:]
            for half in range(2):
                term = edges_cols[:, 6 * half + 2 * n + side, :]
                col_sum[half][side] = term if n == 0 else col_sum[half][side] + term
                at = n * 4 * CTRL + (2 + side) * CTRL
                edges[half * HALF:(half + 1) * HALF, at:at + CTRL] = col_sum[half][side]
    all_edges[pl.ds(me_dsg, 1)] = edges[...][None]
    dsg_start(1, lambda peer: edges, all_edges)
    calm = dot3(mm, jnp.concatenate([tile * total_pair[...] for tile in span], 0), sine_pair[...])
    for t in range(HALF):
        design_out[t] = dot3(mm, sine[...], calm[t * CTRL:(t + 1) * CTRL])
    first_free = dot3(mm, first[...], sine[...])
    pair_first_free = dot3(mm, pair_first[...], sine_pair[...])
    dsg_wait(1, all_edges)

    base = all_edges[...].reshape(PATCHES, 12 * CTRL)

    def exchange(edge):
        taken = []
        for side in range(4):
            other = side ^ 1
            taken.append(exact(mm, facing[side], edge[:, other * CTRL:(other + 1) * CTRL]))
        return jnp.concatenate(taken, 1)

    width = 4 * CTRL
    halo0 = exchange(base[:, 0:width])
    halo1 = exchange(base[:, width:2 * width] + dot3(mm, halo0, spread0[...]))
    halo2 = exchange(
        base[:, 2 * width:] + dot3(mm, halo0, spread1[...]) + dot3(mm, halo1, spread0[...])
    )
    halo[0], halo[1], halo[2] = halo0, halo1, halo2
    halo_rows[...] = jnp.zeros((HALF, 8, LANES), F32)
    halo_cols[...] = jnp.zeros((HALF, 16, CTRL), F32)
    mine = pl.ds(pl.multiple_of(me_dsg * OWN, 8), OWN)
    for k in range(3):
        own = halo[2 - k, mine, :]
        for side in range(2):
            row = 2 * k + side
            at = side * CTRL
            pair = jnp.concatenate([own[0:HALF, at:at + CTRL], own[HALF:OWN, at:at + CTRL]], 1)
            halo_rows[:, row, :] = pair * (SMOOTHING * lane_power[row:row + 1, :])
            at = (2 + side) * CTRL
            for half in range(2):
                halo_cols[:, 6 * half + row, :] = own[half * HALF:(half + 1) * HALF, at:at + CTRL] * (
                    SMOOTHING * pair_power[row:row + 1, :]
                )
    rows_free = dot3(mm, halo_rows[...].reshape(HALF * 8, LANES), sine_pair[...])
    cols_free = dot3(mm, halo_cols[...].reshape(HALF * 16, CTRL), sine[...])
    for t in range(HALF):
        outer = jnp.concatenate([first_free, cols_free[t * 16:(t + 1) * 16]], 0)
        inner = jnp.concatenate([rows_free[t * 8:(t + 1) * 8], pair_first_free], 0)
        design_out[t] += dot3(mm_tn, outer, inner)


def finish(far_ref, pair_ref, far_out, design_out):
    far_out[...] = far_ref[...]
    design_out[0:HALF] = pair_ref[:, :, 0:CTRL]
    design_out[HALF:OWN] = pair_ref[:, :, CTRL:]


def per_device(
    fields, far_geom, far_block, far_cell, far_patch, near_geom, near_cell, near_patch, adjacency
):
    far_count = far_cell.shape[0]
    near_count = near_cell.shape[0]
    points = far_count + near_count
    vmem = pl.BlockSpec(memory_space=pltpu.VMEM)
    smem = pl.BlockSpec(memory_space=pltpu.SMEM)
    stay = pl.BlockSpec(memory_space=pl.ANY)
    tables = [jnp.asarray(t) for t in constants()]
    dma = pltpu.SemaphoreType.DMA
    far, pairs = pl.pallas_call(
        kernel,
        out_shape=(
            jax.ShapeDtypeStruct((1, far_count), F32),
            jax.ShapeDtypeStruct((HALF, CTRL, LANES), F32),
        ),
        in_specs=[vmem] * 5 + [smem] + [vmem] * 2 + [stay] * (1 + len(tables)),
        out_specs=(vmem, vmem),
        scratch_shapes=[pltpu.VMEM(fields.shape, F32)]
        + [pltpu.VMEM(t.shape, F32) for t in tables]
        + [
            pltpu.VMEM((LANES, LANES), F32),
            pltpu.VMEM((CTRL, points), F32),
            pltpu.VMEM((GROUP * CTRL, points), F32),
            pltpu.VMEM((16, LANES), I32),
            pltpu.SMEM((16, LANES), I32),
            pltpu.VMEM((LANES, LANES), F32),
            pltpu.VMEM((VOL, 1, 2 * LANES), F32),
            pltpu.VMEM((VOL, 1, 2 * LANES), F32),
            pltpu.VMEM((VOL, 1, LANES), F32),
            pltpu.VMEM((VOL, 1, LANES), F32),
            pltpu.VMEM((VOL, 1, GROUP * CTRL), F32),
            pltpu.VMEM((VOL, 1, GROUP * CTRL), F32),
            pltpu.VMEM((DSG, 1, ROW), F32),
            pltpu.VMEM((DSG, 1, ROW), F32),
            pltpu.VMEM((1, ROW), F32),
            pltpu.VMEM((VOL_Z, VOL_Y, VOL_C, 1, ROW), F32),
            pltpu.VMEM((OWN, 12 * CTRL), F32),
            pltpu.VMEM((DSG, OWN, 12 * CTRL), F32),
            pltpu.VMEM((3, PATCHES, 4 * CTRL), F32),
            pltpu.VMEM((HALF, 8, LANES), F32),
            pltpu.VMEM((HALF, 16, CTRL), F32),
            dma((3,)), dma((3,)), dma((2,)), dma((2,)),
            dma, dma((VOL_Z,)), dma, dma((VOL_Y,)), dma, dma,
            dma, dma((len(tables),)), dma,
        ],
        compiler_params=pltpu.CompilerParams(
            collective_id=0, has_side_effects=True, vmem_limit_bytes=60000 * 1024
        ),
    )(
        far_geom,
        far_block.reshape(1, far_count),
        far_cell.reshape(1, far_count),
        far_patch.reshape(1, far_count),
        near_geom,
        near_cell.reshape(near_count // LANES, LANES),
        near_patch.reshape(1, near_count),
        adjacency.T,
        fields,
        *tables,
    )
    far, design = pl.pallas_call(
        finish,
        out_shape=(
            jax.ShapeDtypeStruct((1, far_count), F32),
            jax.ShapeDtypeStruct((OWN, CTRL, CTRL), F32),
        ),
        in_specs=[vmem] * 2,
        out_specs=(vmem, vmem),
    )(far, pairs)
    return far.reshape(far_count), design


def solution(mesh):
    return jax.shard_map(
        per_device,
        mesh=mesh,
        in_specs=(
            P("vol", None),
            P(None, ("vol", "dsg")),
            P(("vol", "dsg"), None),
            P(("vol", "dsg")),
            P(("vol", "dsg")),
            P(None, ("vol", "dsg")),
            P(("vol", "dsg")),
            P(("vol", "dsg")),
            P(),
        ),
        out_specs=(P(("vol", "dsg")), P("dsg", None, None)),
        check_vma=False,
    )
```

```python
import jax
import jax.numpy as jnp
import numpy as np
from jax import lax
from jax.experimental import pallas as pl
from jax.experimental.pallas import tpu as pltpu
from jax.sharding import PartitionSpec as P

F32 = jnp.float32
BF16 = jnp.bfloat16
I32 = jnp.int32
MESH = pl.DeviceIdType.MESH

CTRL = 64
GROUP = 4
CAP = 20
PENALTY = 4.0
SMOOTHING = 16.0
LANES = 128
VOL = 64
VOL_C = 2
DSG = 4
PATCHES = 96
OWN = PATCHES // DSG
HALF = OWN // 2
CHUNKS = 3
TILES = HALF // CHUNKS
PIECE = OWN // CHUNKS
SPAN = TILES * LANES
ROW = OWN * CTRL
NOBODY = 999.0


def constants():
    order = np.arange(1, CTRL + 1)
    sine = np.sqrt(2.0 / (CTRL + 1)) * np.sin(np.pi * np.outer(order, order) / (CTRL + 1))
    spectrum = 2.0 - 2.0 * np.cos(np.pi * order / (CTRL + 1))
    inverse = 1.0 / (1.0 + SMOOTHING * spectrum)
    power = [inverse * (1.0 - inverse) ** k for k in range(4)]
    ends = [sine[0], sine[-1]]
    zero = np.zeros((CTRL, CTRL))
    sine_pair = np.block([[sine, zero], [zero, sine]])
    total = sum(np.outer(p, p) for p in power)
    total_pair = np.concatenate([total, total], 1)

    def spread(k):
        scale = SMOOTHING * np.outer(power[k], power[k])
        table = np.zeros((4, CTRL, 4, CTRL))
        for side in range(4):
            for at in range(CTRL):
                unit = np.zeros(CTRL)
                unit[at] = 1.0
                end = ends[side % 2]
                field = scale * (np.outer(end, unit) if side < 2 else np.outer(unit, end))
                table[side, at, 0] = ends[0] @ field
                table[side, at, 1] = ends[1] @ field
                table[side, at, 2] = field @ ends[0]
                table[side, at, 3] = field @ ends[1]
        return table.reshape(4 * CTRL, 4 * CTRL)

    first = np.zeros((8, CTRL))
    lane_power = np.zeros((8, LANES))
    pair_first = np.zeros((16, LANES))
    pair_power = np.zeros((16, CTRL))
    for k in range(3):
        for side in range(2):
            row = 2 * k + side
            first[row] = power[k] * ends[side]
            lane_power[row] = np.tile(power[k], 2)
            for half in range(2):
                pair_first[6 * half + row, half * CTRL:(half + 1) * CTRL] = power[k] * ends[side]
                pair_power[6 * half + row] = power[k]
    by_core = np.concatenate([np.arange(core, VOL, VOL_C) for core in range(VOL_C)])
    tables = (sine, sine[:, by_core], sine_pair, total_pair, spread(0), spread(1), first, lane_power, pair_first, pair_power)
    return [np.asarray(t, np.float32) for t in tables]


def iota(shape, axis):
    return lax.broadcasted_iota(I32, shape, axis)


def mm(a, b):
    return jnp.dot(a, b, preferred_element_type=F32)


def mm_nt(a, b):
    return lax.dot_general(a, b, (((1,), (1,)), ((), ())), preferred_element_type=F32)


def mm_tn(a, b):
    return lax.dot_general(a, b, (((0,), (0,)), ((), ())), preferred_element_type=F32)


def split2(x):
    high = x.astype(BF16)
    return high, (x - high.astype(F32)).astype(BF16)


def split3(x):
    high = x.astype(BF16)
    rest = x - high.astype(F32)
    middle = rest.astype(BF16)
    return high, middle, (rest - middle.astype(F32)).astype(BF16)


def exact(product, picks, x):
    high, middle, low = split3(x)
    picks = picks.astype(BF16)
    return product(picks, high) + product(picks, middle) + product(picks, low)


def dot3(product, a, b):
    a_high, a_low = split2(a)
    b_high, b_low = split2(b)
    return product(a_high, b_high) + product(a_high, b_low) + product(a_low, b_high)


def bernstein(t):
    c = 1.0 - t
    values = [c * c * c, 3.0 * t * c * c, 3.0 * t * t * c, t * t * t]
    slopes = [-3.0 * c * c, 3.0 * c * c - 6.0 * t * c, 6.0 * t * c - 3.0 * t * t, 3.0 * t * t]
    return values, slopes


def pick(index, rows):
    return jnp.where(
        index == 0, rows[0], jnp.where(index == 1, rows[1], jnp.where(index == 2, rows[2], rows[3]))
    )


def densities(columns, coords, normals):
    count = columns.shape[1]
    value_x, slope_x = bernstein(coords[0])
    value_y, slope_y = bernstein(coords[1])
    value_z, slope_z = bernstein(coords[2])
    place = iota((16, count), 0)
    at_y, at_z = place // 4, place % 4
    value_y, slope_y = pick(at_y, value_y), pick(at_y, slope_y)
    value_z, slope_z = pick(at_z, value_z), pick(at_z, slope_z)
    plain, with_y, with_z = value_y * value_z, slope_y * value_z, value_y * slope_z
    point = []
    for base in (0, 64):
        parts = [columns[base + 16 * i:base + 16 * i + 16] for i in range(4)]
        value = parts[0] * value_x[0] + parts[1] * value_x[1] + parts[2] * value_x[2] + parts[3] * value_x[3]
        slope = parts[0] * slope_x[0] + parts[1] * slope_x[1] + parts[2] * slope_x[2] + parts[3] * slope_x[3]
        products = (value * plain, slope * plain, value * with_y, value * with_z)
        point.append([jnp.sum(product, 0, keepdims=True) for product in products])
    (u, ux, uy, uz), (w, wx, wy, wz) = point
    nx, ny, nz = normals
    squared = nx * nx + ny * ny + nz * nz
    inner = ux * wx + uy * wy + uz * wz
    along_u = ux * nx + uy * ny + uz * nz
    along_w = wx * nx + wy * ny + wz * nz
    return squared * inner - 2.0 * along_u * along_w + PENALTY * squared * u * w


def spline(param):
    scaled = param * (CTRL - 3.0)
    start = jnp.clip(jnp.floor(scaled), 0.0, CTRL - 4.0)
    x = scaled - start
    c = 1.0 - x
    square, cube = x * x, x * x * x
    weights = (
        c * c * c / 6.0,
        (3.0 * cube - 6.0 * square + 4.0) / 6.0,
        (-3.0 * cube + 3.0 * square + 3.0 * x + 1.0) / 6.0,
        cube / 6.0,
    )
    offset = iota((CTRL, param.shape[1]), 0) - start.astype(I32)
    result = jnp.where(offset == 3, weights[3], 0.0)
    for k in (2, 1, 0):
        result = jnp.where(offset == k, weights[k], result)
    return result


def kernel(
    far_geom, block, far_cell, far_patch, near_geom, near_cell, near_patch, adjacency,
    fields_in, sine_in, sine_rows_in, sine_pair_in, total_pair_in, spread0_in, spread1_in, first_in, lane_power_in,
    pair_first_in, pair_power_in,
    far_out, design_out,
    fields, sine, sine_rows, sine_pair, total_pair, spread0, spread1, first, lane_power, pair_first, pair_power,
    rows, left, right, cells_v, cells_s, dens, ask, asked, reply, replied, grid, grids, part, parts,
    line, lines, edges, all_edges, halo, halo_rows, halo_cols,
    vol_send, vol_recv, dsg_send, dsg_recv, row_send, row_recv, core_send, core_recv,
    local_sem, load_sem, fields_sem,
):
    me_vol = lax.axis_index("vol")
    me_dsg = lax.axis_index("dsg")
    far_count = far_geom.shape[1]
    near_count = near_geom.shape[1]

    load_fields = pltpu.make_async_copy(fields_in, fields, fields_sem)
    load_fields.start()
    loads = [
        pltpu.make_async_copy(source, target, load_sem.at[i])
        for i, (source, target) in enumerate(
            (
                (sine_in, sine), (sine_rows_in, sine_rows), (sine_pair_in, sine_pair), (total_pair_in, total_pair),
                (spread0_in, spread0), (spread1_in, spread1), (first_in, first),
                (lane_power_in, lane_power), (pair_first_in, pair_first), (pair_power_in, pair_power),
            )
        )
    ]
    for load in loads:
        load.start()

    barrier = pltpu.get_barrier_semaphore()

    def greet_vol(t, carry):
        peer = jnp.where(me_vol + t >= VOL, me_vol + t - VOL, me_vol + t)
        pl.semaphore_signal(barrier, inc=1, device_id={"vol": peer}, device_id_type=MESH)
        return carry

    lax.fori_loop(1, VOL, greet_vol, 0)
    for t in range(1, DSG):
        peer = jnp.where(me_dsg + t >= DSG, me_dsg + t - DSG, me_dsg + t)
        pl.semaphore_signal(barrier, inc=1, device_id={"dsg": peer}, device_id_type=MESH)

    def wrap(index, size):
        return jnp.where(index >= size, index - size, index)

    def vol_start(phase, source, target):
        def step(t, carry):
            peer = wrap(me_vol + t, VOL)
            pltpu.make_async_remote_copy(
                src_ref=source.at[peer],
                dst_ref=target.at[me_vol],
                send_sem=vol_send.at[phase],
                recv_sem=vol_recv.at[phase],
                device_id={"vol": peer},
                device_id_type=MESH,
            ).start()
            return carry

        lax.fori_loop(1, VOL, step, 0)

    def settle(ref, sem):
        pltpu.make_async_copy(ref, ref, sem).wait()

    def vol_wait(phase, source, target):
        settle(target.at[pl.ds(0, VOL - 1)], vol_recv.at[phase])
        settle(source.at[pl.ds(0, VOL - 1)], vol_send.at[phase])

    def dsg_start(phase, source, target):
        for t in (2, 1, 3):
            peer = wrap(me_dsg + t, DSG)
            pltpu.make_async_remote_copy(
                src_ref=source(peer),
                dst_ref=target.at[me_dsg],
                send_sem=dsg_send.at[phase],
                recv_sem=dsg_recv.at[phase],
                device_id={"dsg": peer},
                device_id_type=MESH,
            ).start()

    def dsg_wait(phase, target):
        settle(target.at[pl.ds(0, DSG - 1)], dsg_recv.at[phase])
        settle(target.at[pl.ds(0, DSG - 1)], dsg_send.at[phase])

    unseen = jnp.int32(PATCHES)
    near_ids, far_ids = near_patch[...], far_patch[...]
    ids = []
    previous = None
    for _ in range(GROUP):
        if previous is None:
            near_left, far_left = near_ids, far_ids
        else:
            near_left = jnp.where(near_ids > previous, near_ids, unseen)
            far_left = jnp.where(far_ids > previous, far_ids, unseen)
        previous = jnp.minimum(
            jnp.min(near_left, 1, keepdims=True), jnp.min(far_left, 1, keepdims=True)
        )
        ids.append(previous)

    to_block = iota((VOL, far_count), 0) == block[...]
    to_block_f = jnp.where(to_block, 1.0, 0.0)
    to_block_b = to_block_f.astype(BF16)
    earlier = jnp.where(
        iota((far_count, far_count), 0) < iota((far_count, far_count), 1), 1.0, 0.0
    ).astype(BF16)
    rank = jnp.sum(mm(to_block_b, earlier) * to_block_f, 0, keepdims=True).astype(I32)
    values = jnp.concatenate(
        [far_cell[...].astype(F32), far_geom[0:6, :], jnp.zeros((1, far_count), F32)], 0
    )
    placed = [jnp.where(rank == r, values, 0.0) for r in range(CAP)]
    placed.append(jnp.zeros((2 * LANES - 8 * CAP, far_count), F32))
    request = exact(mm_nt, to_block_b, jnp.concatenate(placed, 0))
    lane = iota((VOL, 2 * LANES), 1)
    for s in range(GROUP):
        request = jnp.where(lane == 8 * CAP + s, ids[s].astype(F32), request)
    ask[:, 0, :] = request
    asked[pl.ds(me_vol, 1)] = ask[pl.ds(me_vol, 1)]

    sides = jnp.concatenate(
        [jnp.concatenate([adjacency[...], jnp.full((4, LANES - PATCHES), -1, I32)], 1)] * 2, 0
    ).astype(F32).T[0:PATCHES]
    patch_lane = iota((PATCHES, PATCHES), 1).astype(F32)
    facing = [jnp.where(patch_lane == sides[:, side:side + 1], 1.0, 0.0).astype(BF16) for side in range(4)]


    def take(cells, t, slot, bounded=False):
        for r in range(LANES):
            cell = jnp.clip(cells[t, r], 0, fields.shape[0] - 1) if bounded else cells[t, r]
            rows[slot, r:r + 1, :] = fields[pl.ds(cell, 1), :]
        return rows[slot].T

    def scatter(at, strength, s_param, t_param, patch):
        left[:, pl.ds(at, LANES)] = spline(s_param)
        weights = spline(t_param)
        if strength is not None:
            weights = weights * strength
        for s in range(GROUP):
            right[s * CTRL:(s + 1) * CTRL, pl.ds(at, LANES)] = jnp.where(patch == ids[s], weights, 0.0)

    def near_chunk(t, carry):
        at = pl.multiple_of(t * LANES, LANES)
        columns = take(near_cell, t, 0)
        geom = near_geom[:, pl.ds(at, LANES)]
        strength = densities(
            columns, [geom[i:i + 1] for i in range(3)], [geom[i:i + 1] for i in range(3, 6)]
        )
        scatter(at, strength, geom[6:7], geom[7:8], near_patch[:, pl.ds(at, LANES)])
        return carry

    load_fields.wait()
    chunks = near_count // LANES
    lax.fori_loop(0, chunks // 4, near_chunk, 0)

    pl.semaphore_wait(barrier, VOL - 1 + DSG - 1)
    vol_start(0, ask, asked)
    lax.fori_loop(chunks // 4, 5 * chunks // 8, near_chunk, 0)

    vol_wait(0, ask, asked)
    wanted = asked[:, 0, :].T
    tiles = []
    for t in range(CAP // 2):
        one = wanted[16 * t:16 * t + 8]
        two = wanted[16 * t + 8:16 * t + 16]
        tiles.append(jnp.concatenate([one, two], 1))
    cells_v[...] = jnp.concatenate(
        [jnp.clip((tile[0:1] + 0.5).astype(I32), 0, fields.shape[0] - 1) for tile in tiles] + [jnp.zeros((16 - CAP // 2, LANES), I32)], 0
    )
    to_scalar = pltpu.make_async_copy(cells_v, cells_s, local_sem)
    to_scalar.start()
    to_scalar.wait()
    dens[...] = jnp.zeros((LANES, LANES), F32)
    for t in range(CAP // 2):
        columns = take(cells_s, t, t % 4, True)
        tile = tiles[t]
        strength = densities(
            columns, [tile[i:i + 1] for i in range(1, 4)], [tile[i:i + 1] for i in range(4, 7)]
        )
        dens[2 * t:2 * t + 1, 0:VOL] = strength[:, 0:VOL]
        dens[2 * t + 1:2 * t + 2, 0:VOL] = strength[:, VOL:]
    reply[:, 0, :] = dens[...].T[0:VOL, :]
    replied[pl.ds(me_vol, 1)] = reply[pl.ds(me_vol, 1)]
    vol_start(1, reply, replied)

    lax.fori_loop(5 * chunks // 8, chunks, near_chunk, 0)
    near_grid = dot3(mm_nt, left[:, 0:near_count], right[:, 0:near_count])

    for t in range(far_count // LANES):
        at = slice(t * LANES, (t + 1) * LANES)
        scatter(near_count + t * LANES, None, far_geom[6:7, at], far_geom[7:8, at], far_patch[:, at])
    far_right, far_right_low = split2(right[:, near_count:])
    patch_of = iota((PATCHES, VOL), 0).astype(F32)
    places = [
        jnp.where(patch_of == wanted[8 * CAP + s:8 * CAP + s + 1, :], 1.0, 0.0).astype(BF16)
        for s in range(GROUP)
    ]
    vol_wait(1, reply, replied)
    answers = replied[:, 0, :].T
    high, middle, low = split3(answers)
    by_rank = mm(high, to_block_b) + mm(middle, to_block_b) + mm(low, to_block_b)
    far_strength = jnp.sum(
        jnp.where(iota((LANES, far_count), 0) == rank, by_rank, 0.0), 0, keepdims=True
    )
    far_out[...] = far_strength
    far_left, far_left_low = split2(left[:, near_count:] * far_strength)
    grid[:, 0, :] = (
        near_grid
        + mm_nt(far_left, far_right)
        + mm_nt(far_left, far_right_low)
        + mm_nt(far_left_low, far_right)
    )
    grids[pl.ds(me_vol, 1)] = grid[pl.ds(me_vol, 1)]
    vol_start(2, grid, grids)
    vol_wait(2, grid, grids)

    got = grids[:, 0, :]
    total = None
    for s in range(GROUP):
        term = exact(mm, places[s], got[:, s * CTRL:(s + 1) * CTRL])
        total = term if total is None else total + term
    loads[0].wait()
    total = dot3(mm, total, sine[...])
    for owner in range(DSG):
        base = owner * OWN
        for t in range(HALF):
            low = base + t // TILES * PIECE + t % TILES
            part[owner, :, t * LANES:t * LANES + CTRL] = total[low:low + 1]
            part[owner, :, t * LANES + CTRL:(t + 1) * LANES] = total[low + TILES:low + TILES + 1]
    parts[pl.ds(me_dsg, 1)] = part[pl.ds(me_dsg, 1)]
    dsg_start(0, lambda peer: part.at[peer], parts)
    dsg_wait(0, parts)
    summed = parts[0] + parts[1] + parts[2] + parts[3]
    me_core, me_chip = me_vol % VOL_C, me_vol // VOL_C
    for c in range(CHUNKS):
        line[c] = summed[:, c * SPAN:(c + 1) * SPAN]
        lines[c, me_core, me_chip] = line[c]
    for c in range(CHUNKS):

        def fan(t, carry, c=c):
            pltpu.make_async_remote_copy(
                src_ref=line.at[c],
                dst_ref=lines.at[c, me_core, me_chip],
                send_sem=row_send.at[c],
                recv_sem=row_recv.at[c],
                device_id={"vol": wrap(me_vol + VOL_C * t, VOL)},
                device_id_type=MESH,
            ).start()
            return carry

        lax.fori_loop(1, VOL // VOL_C, fan, 0)

    def hand_over(c):
        settle(lines.at[c, 0, pl.ds(0, VOL // VOL_C - 1)], row_recv.at[c])
        pltpu.make_async_remote_copy(
            src_ref=lines.at[c, me_core],
            dst_ref=lines.at[c, me_core],
            send_sem=core_send.at[c],
            recv_sem=core_recv.at[c],
            device_id={"vol": me_chip * VOL_C + 1 - me_core},
            device_id_type=MESH,
        ).start()

    span = []

    def edges_of(c):
        settle(lines.at[c, 0], core_recv.at[c])
        whole = dot3(mm, sine_rows[...], lines[c].reshape(VOL, SPAN))
        tiles_here = [whole[:, t * LANES:(t + 1) * LANES] for t in range(TILES)]
        span.extend(tiles_here)
        across = dot3(mm, first[...], whole)
        across = jnp.concatenate(
            [across[:, t * LANES:(t + 1) * LANES] * lane_power[...] for t in range(TILES)], 0
        ).reshape(TILES, 8, LANES)
        along = jnp.concatenate(
            [dot3(mm_nt, pair_first[...], tile) * pair_power[...] for tile in tiles_here], 0
        ).reshape(TILES, 16, CTRL)
        row_sum = [None, None]
        col_sum = [[None, None], [None, None]]
        for n in range(3):
            for side in range(2):
                term = across[:, 2 * n + side, :]
                row_sum[side] = term if n == 0 else row_sum[side] + term
                at = n * 4 * CTRL + side * CTRL
                edges[c, 0:TILES, at:at + CTRL] = row_sum[side][:, 0:CTRL]
                edges[c, TILES:PIECE, at:at + CTRL] = row_sum[side][:, CTRL:]
                for half in range(2):
                    term = along[:, 6 * half + 2 * n + side, :]
                    col_sum[half][side] = term if n == 0 else col_sum[half][side] + term
                    at = n * 4 * CTRL + (2 + side) * CTRL
                    edges[c, half * TILES:(half + 1) * TILES, at:at + CTRL] = col_sum[half][side]
        all_edges[c, pl.ds(me_dsg, 1)] = edges[c][None]
        dsg_start(1 + c, lambda peer: edges.at[c], all_edges.at[c])

    for load in loads[1:]:
        load.wait()
    hand_over(0)
    hand_over(1)
    edges_of(0)
    hand_over(2)
    edges_of(1)
    edges_of(2)
    for c in range(CHUNKS):
        settle(lines.at[c, 0, pl.ds(0, VOL // VOL_C - 1)], row_send.at[c])
        settle(lines.at[c, 0], core_send.at[c])

    calm = dot3(mm, jnp.concatenate([tile * total_pair[...] for tile in span], 0), sine_pair[...])
    for t in range(HALF):
        design_out[t] = dot3(mm, sine[...], calm[t * CTRL:(t + 1) * CTRL])
    first_free = dot3(mm, first[...], sine[...])
    pair_first_free = dot3(mm, pair_first[...], sine_pair[...])
    for c in range(CHUNKS):
        dsg_wait(1 + c, all_edges.at[c])

    base = jnp.concatenate([all_edges[c, owner] for owner in range(DSG) for c in range(CHUNKS)], 0)

    def exchange(edge):
        taken = []
        for side in range(4):
            other = side ^ 1
            taken.append(exact(mm, facing[side], edge[:, other * CTRL:(other + 1) * CTRL]))
        return jnp.concatenate(taken, 1)

    width = 4 * CTRL
    halo0 = exchange(base[:, 0:width])
    halo1 = exchange(base[:, width:2 * width] + dot3(mm, halo0, spread0[...]))
    halo2 = exchange(
        base[:, 2 * width:] + dot3(mm, halo0, spread1[...]) + dot3(mm, halo1, spread0[...])
    )
    halo[0], halo[1], halo[2] = halo0, halo1, halo2
    halo_rows[...] = jnp.zeros((HALF, 8, LANES), F32)
    halo_cols[...] = jnp.zeros((HALF, 16, CTRL), F32)
    mine = pl.ds(pl.multiple_of(me_dsg * OWN, 8), OWN)
    for k in range(3):
        own = halo[2 - k, mine, :]
        for side in range(2):
            row = 2 * k + side
            for c in range(CHUNKS):
                here = slice(c * TILES, (c + 1) * TILES)
                halves = [own[c * PIECE + half * TILES:c * PIECE + (half + 1) * TILES] for half in range(2)]
                at = side * CTRL
                pair = jnp.concatenate([half[:, at:at + CTRL] for half in halves], 1)
                halo_rows[here, row, :] = pair * (SMOOTHING * lane_power[row:row + 1, :])
                at = (2 + side) * CTRL
                for half in range(2):
                    halo_cols[here, 6 * half + row, :] = halves[half][:, at:at + CTRL] * (
                        SMOOTHING * pair_power[row:row + 1, :]
                    )
    rows_free = dot3(mm, halo_rows[...].reshape(HALF * 8, LANES), sine_pair[...])
    cols_free = dot3(mm, halo_cols[...].reshape(HALF * 16, CTRL), sine[...])
    for t in range(HALF):
        outer = jnp.concatenate([first_free, cols_free[t * 16:(t + 1) * 16]], 0)
        inner = jnp.concatenate([rows_free[t * 8:(t + 1) * 8], pair_first_free], 0)
        design_out[t] += dot3(mm_tn, outer, inner)


def finish(far_ref, pair_ref, far_out, design_out):
    far_out[...] = far_ref[...]
    for c in range(CHUNKS):
        for half in range(2):
            at = c * PIECE + half * TILES
            design_out[at:at + TILES] = pair_ref[
                c * TILES:(c + 1) * TILES, :, half * CTRL:(half + 1) * CTRL
            ]


def per_device(
    fields, far_geom, far_block, far_cell, far_patch, near_geom, near_cell, near_patch, adjacency
):
    far_count = far_cell.shape[0]
    near_count = near_cell.shape[0]
    points = far_count + near_count
    vmem = pl.BlockSpec(memory_space=pltpu.VMEM)
    smem = pl.BlockSpec(memory_space=pltpu.SMEM)
    stay = pl.BlockSpec(memory_space=pl.ANY)
    tables = [jnp.asarray(t) for t in constants()]
    dma = pltpu.SemaphoreType.DMA
    far, pairs = pl.pallas_call(
        kernel,
        out_shape=(
            jax.ShapeDtypeStruct((1, far_count), F32),
            jax.ShapeDtypeStruct((HALF, CTRL, LANES), F32),
        ),
        in_specs=[vmem] * 5 + [smem] + [vmem] * 2 + [stay] * (1 + len(tables)),
        out_specs=(vmem, vmem),
        scratch_shapes=[pltpu.VMEM(fields.shape, F32)]
        + [pltpu.VMEM(t.shape, F32) for t in tables]
        + [
            pltpu.VMEM((4, LANES, LANES), F32),
            pltpu.VMEM((CTRL, points), F32),
            pltpu.VMEM((GROUP * CTRL, points), F32),
            pltpu.VMEM((16, LANES), I32),
            pltpu.SMEM((16, LANES), I32),
            pltpu.VMEM((LANES, LANES), F32),
            pltpu.VMEM((VOL, 1, 2 * LANES), F32),
            pltpu.VMEM((VOL, 1, 2 * LANES), F32),
            pltpu.VMEM((VOL, 1, LANES), F32),
            pltpu.VMEM((VOL, 1, LANES), F32),
            pltpu.VMEM((VOL, 1, GROUP * CTRL), F32),
            pltpu.VMEM((VOL, 1, GROUP * CTRL), F32),
            pltpu.VMEM((DSG, 1, ROW), F32),
            pltpu.VMEM((DSG, 1, ROW), F32),
            pltpu.VMEM((CHUNKS, 1, SPAN), F32),
            pltpu.VMEM((CHUNKS, VOL_C, VOL // VOL_C, 1, SPAN), F32),
            pltpu.VMEM((CHUNKS, PIECE, 12 * CTRL), F32),
            pltpu.VMEM((CHUNKS, DSG, PIECE, 12 * CTRL), F32),
            pltpu.VMEM((3, PATCHES, 4 * CTRL), F32),
            pltpu.VMEM((HALF, 8, LANES), F32),
            pltpu.VMEM((HALF, 16, CTRL), F32),
            dma((3,)), dma((3,)), dma((1 + CHUNKS,)), dma((1 + CHUNKS,)),
            dma((CHUNKS,)), dma((CHUNKS,)), dma((CHUNKS,)), dma((CHUNKS,)),
            dma, dma((len(tables),)), dma,
        ],
        compiler_params=pltpu.CompilerParams(
            collective_id=0, has_side_effects=True, vmem_limit_bytes=60000 * 1024
        ),
    )(
        far_geom,
        far_block.reshape(1, far_count),
        far_cell.reshape(1, far_count),
        far_patch.reshape(1, far_count),
        near_geom,
        near_cell.reshape(near_count // LANES, LANES),
        near_patch.reshape(1, near_count),
        adjacency.T,
        fields,
        *tables,
    )
    far, design = pl.pallas_call(
        finish,
        out_shape=(
            jax.ShapeDtypeStruct((1, far_count), F32),
            jax.ShapeDtypeStruct((OWN, CTRL, CTRL), F32),
        ),
        in_specs=[vmem] * 2,
        out_specs=(vmem, vmem),
    )(far, pairs)
    return far.reshape(far_count), design


def solution(mesh):
    return jax.shard_map(
        per_device,
        mesh=mesh,
        in_specs=(
            P("vol", None),
            P(None, ("vol", "dsg")),
            P(("vol", "dsg"), None),
            P(("vol", "dsg")),
            P(("vol", "dsg")),
            P(None, ("vol", "dsg")),
            P(("vol", "dsg")),
            P(("vol", "dsg")),
            P(),
        ),
        out_specs=(P(("vol", "dsg")), P("dsg", None, None)),
        check_vma=False,
    )
```

```python
import jax
import jax.numpy as jnp
import numpy as np
from jax import lax
from jax.experimental import pallas as pl
from jax.experimental.pallas import tpu as pltpu
from jax.sharding import PartitionSpec as P

F32 = jnp.float32
BF16 = jnp.bfloat16
I32 = jnp.int32
MESH = pl.DeviceIdType.MESH

CTRL = 64
GROUP = 4
CAP = 20
PENALTY = 4.0
SMOOTHING = 16.0
LANES = 128
VOL = 64
VOL_C = 2
DSG = 4
PATCHES = 96
OWN = PATCHES // DSG
HALF = OWN // 2
CHUNKS = 3
TILES = HALF // CHUNKS
PIECE = OWN // CHUNKS
SPAN = TILES * LANES
ROW = OWN * CTRL
NOBODY = 999.0


def constants():
    order = np.arange(1, CTRL + 1)
    sine = np.sqrt(2.0 / (CTRL + 1)) * np.sin(np.pi * np.outer(order, order) / (CTRL + 1))
    spectrum = 2.0 - 2.0 * np.cos(np.pi * order / (CTRL + 1))
    inverse = 1.0 / (1.0 + SMOOTHING * spectrum)
    power = [inverse * (1.0 - inverse) ** k for k in range(4)]
    ends = [sine[0], sine[-1]]
    zero = np.zeros((CTRL, CTRL))
    sine_pair = np.block([[sine, zero], [zero, sine]])
    total = sum(np.outer(p, p) for p in power)
    total_pair = np.concatenate([total, total], 1)

    def spread(k):
        scale = SMOOTHING * np.outer(power[k], power[k])
        table = np.zeros((4, CTRL, 4, CTRL))
        for side in range(4):
            for at in range(CTRL):
                unit = np.zeros(CTRL)
                unit[at] = 1.0
                end = ends[side % 2]
                field = scale * (np.outer(end, unit) if side < 2 else np.outer(unit, end))
                table[side, at, 0] = ends[0] @ field
                table[side, at, 1] = ends[1] @ field
                table[side, at, 2] = field @ ends[0]
                table[side, at, 3] = field @ ends[1]
        return table.reshape(4 * CTRL, 4 * CTRL)

    first = np.zeros((8, CTRL))
    lane_power = np.zeros((8, LANES))
    pair_first = np.zeros((16, LANES))
    pair_power = np.zeros((16, CTRL))
    for k in range(3):
        for side in range(2):
            row = 2 * k + side
            first[row] = power[k] * ends[side]
            lane_power[row] = np.tile(power[k], 2)
            for half in range(2):
                pair_first[6 * half + row, half * CTRL:(half + 1) * CTRL] = power[k] * ends[side]
                pair_power[6 * half + row] = power[k]
    held = np.arange(VOL)
    held = held % VOL_C * (VOL // VOL_C) + held // VOL_C
    tables = (sine, sine[held], sine_pair, total_pair, spread(0), spread(1), first, lane_power, pair_first, pair_power)
    return [np.asarray(t, np.float32) for t in tables]


def iota(shape, axis):
    return lax.broadcasted_iota(I32, shape, axis)


def mm(a, b):
    return jnp.dot(a, b, preferred_element_type=F32)


def mm_nt(a, b):
    return lax.dot_general(a, b, (((1,), (1,)), ((), ())), preferred_element_type=F32)


def mm_tn(a, b):
    return lax.dot_general(a, b, (((0,), (0,)), ((), ())), preferred_element_type=F32)


def split2(x):
    high = x.astype(BF16)
    return high, (x - high.astype(F32)).astype(BF16)


def split3(x):
    high = x.astype(BF16)
    rest = x - high.astype(F32)
    middle = rest.astype(BF16)
    return high, middle, (rest - middle.astype(F32)).astype(BF16)


def exact(product, picks, x):
    high, middle, low = split3(x)
    picks = picks.astype(BF16)
    return product(picks, high) + product(picks, middle) + product(picks, low)


def picked(product, picks, x):
    high, low = split2(x)
    return product(picks, high) + product(picks, low)


def dot3(product, a, b):
    a_high, a_low = split2(a)
    b_high, b_low = split2(b)
    return product(a_high, b_high) + product(a_high, b_low) + product(a_low, b_high)


def bernstein(t):
    c = 1.0 - t
    values = [c * c * c, 3.0 * t * c * c, 3.0 * t * t * c, t * t * t]
    slopes = [-3.0 * c * c, 3.0 * c * c - 6.0 * t * c, 6.0 * t * c - 3.0 * t * t, 3.0 * t * t]
    return values, slopes


def pick(index, rows):
    return jnp.where(
        index == 0, rows[0], jnp.where(index == 1, rows[1], jnp.where(index == 2, rows[2], rows[3]))
    )


def densities(columns, coords, normals):
    count = columns.shape[1]
    value_x, slope_x = bernstein(coords[0])
    value_y, slope_y = bernstein(coords[1])
    value_z, slope_z = bernstein(coords[2])
    place = iota((16, count), 0)
    at_y, at_z = place // 4, place % 4
    value_y, slope_y = pick(at_y, value_y), pick(at_y, slope_y)
    value_z, slope_z = pick(at_z, value_z), pick(at_z, slope_z)
    plain, with_y, with_z = value_y * value_z, slope_y * value_z, value_y * slope_z
    point = []
    for base in (0, 64):
        parts = [columns[base + 16 * i:base + 16 * i + 16] for i in range(4)]
        value = parts[0] * value_x[0] + parts[1] * value_x[1] + parts[2] * value_x[2] + parts[3] * value_x[3]
        slope = parts[0] * slope_x[0] + parts[1] * slope_x[1] + parts[2] * slope_x[2] + parts[3] * slope_x[3]
        products = (value * plain, slope * plain, value * with_y, value * with_z)
        point.append([jnp.sum(product, 0, keepdims=True) for product in products])
    (u, ux, uy, uz), (w, wx, wy, wz) = point
    nx, ny, nz = normals
    squared = nx * nx + ny * ny + nz * nz
    inner = ux * wx + uy * wy + uz * wz
    along_u = ux * nx + uy * ny + uz * nz
    along_w = wx * nx + wy * ny + wz * nz
    return squared * inner - 2.0 * along_u * along_w + PENALTY * squared * u * w


def spline(param):
    scaled = param * (CTRL - 3.0)
    start = jnp.clip(jnp.floor(scaled), 0.0, CTRL - 4.0)
    x = scaled - start
    c = 1.0 - x
    square, cube = x * x, x * x * x
    weights = (
        c * c * c / 6.0,
        (3.0 * cube - 6.0 * square + 4.0) / 6.0,
        (-3.0 * cube + 3.0 * square + 3.0 * x + 1.0) / 6.0,
        cube / 6.0,
    )
    offset = iota((CTRL, param.shape[1]), 0) - start.astype(I32)
    result = jnp.where(offset == 3, weights[3], 0.0)
    for k in (2, 1, 0):
        result = jnp.where(offset == k, weights[k], result)
    return result


def kernel(
    far_geom, block, far_cell, far_patch, near_geom, near_cell, near_patch, adjacency,
    fields_in, sine_in, sine_held_in, sine_pair_in, total_pair_in, spread0_in, spread1_in, first_in, lane_power_in,
    pair_first_in, pair_power_in,
    far_out, design_out,
    fields, sine, sine_held, sine_pair, total_pair, spread0, spread1, first, lane_power, pair_first, pair_power,
    rows, left, right, cells_v, cells_s, dens, ask, asked, reply, replied, grid, grids, part, parts,
    line, lines, edges, all_edges, halo, halo_rows, halo_cols,
    vol_send, vol_recv, dsg_send, dsg_recv, row_send, row_recv, core_send, core_recv,
    local_sem, load_sem, fields_sem,
):
    me_vol = lax.axis_index("vol")
    me_dsg = lax.axis_index("dsg")
    far_count = far_geom.shape[1]
    near_count = near_geom.shape[1]

    load_fields = pltpu.make_async_copy(fields_in, fields, fields_sem)
    load_fields.start()
    loads = [
        pltpu.make_async_copy(source, target, load_sem.at[i])
        for i, (source, target) in enumerate(
            (
                (sine_in, sine), (sine_held_in, sine_held), (sine_pair_in, sine_pair), (total_pair_in, total_pair),
                (spread0_in, spread0), (spread1_in, spread1), (first_in, first),
                (lane_power_in, lane_power), (pair_first_in, pair_first), (pair_power_in, pair_power),
            )
        )
    ]
    for load in loads:
        load.start()

    barrier = pltpu.get_barrier_semaphore()

    def greet_vol(t, carry):
        peer = jnp.where(me_vol + t >= VOL, me_vol + t - VOL, me_vol + t)
        pl.semaphore_signal(barrier, inc=1, device_id={"vol": peer}, device_id_type=MESH)
        return carry

    lax.fori_loop(1, VOL, greet_vol, 0)
    for t in range(1, DSG):
        peer = jnp.where(me_dsg + t >= DSG, me_dsg + t - DSG, me_dsg + t)
        pl.semaphore_signal(barrier, inc=1, device_id={"dsg": peer}, device_id_type=MESH)

    def wrap(index, size):
        return jnp.where(index >= size, index - size, index)

    def vol_start(phase, source, target):
        def step(t, carry):
            peer = wrap(me_vol + t, VOL)
            pltpu.make_async_remote_copy(
                src_ref=source.at[peer],
                dst_ref=target.at[me_vol],
                send_sem=vol_send.at[phase],
                recv_sem=vol_recv.at[phase],
                device_id={"vol": peer},
                device_id_type=MESH,
            ).start()
            return carry

        lax.fori_loop(1, VOL, step, 0)

    def settle(ref, sem):
        pltpu.make_async_copy(ref, ref, sem).wait()

    def vol_wait(phase, source, target):
        settle(target.at[pl.ds(0, VOL - 1)], vol_recv.at[phase])
        settle(source.at[pl.ds(0, VOL - 1)], vol_send.at[phase])

    def dsg_start(phase, source, target):
        for t in (2, 1, 3):
            peer = wrap(me_dsg + t, DSG)
            pltpu.make_async_remote_copy(
                src_ref=source(peer),
                dst_ref=target.at[me_dsg],
                send_sem=dsg_send.at[phase],
                recv_sem=dsg_recv.at[phase],
                device_id={"dsg": peer},
                device_id_type=MESH,
            ).start()

    def dsg_wait(phase, target):
        settle(target.at[pl.ds(0, DSG - 1)], dsg_recv.at[phase])
        settle(target.at[pl.ds(0, DSG - 1)], dsg_send.at[phase])

    unseen = jnp.int32(PATCHES)
    near_ids, far_ids = near_patch[...], far_patch[...]
    ids = []
    previous = None
    for _ in range(GROUP):
        if previous is None:
            near_left, far_left = near_ids, far_ids
        else:
            near_left = jnp.where(near_ids > previous, near_ids, unseen)
            far_left = jnp.where(far_ids > previous, far_ids, unseen)
        previous = jnp.minimum(
            jnp.min(near_left, 1, keepdims=True), jnp.min(far_left, 1, keepdims=True)
        )
        ids.append(previous)

    to_block = iota((VOL, far_count), 0) == block[...]
    to_block_f = jnp.where(to_block, 1.0, 0.0)
    to_block_b = to_block_f.astype(BF16)
    earlier = jnp.where(
        iota((far_count, far_count), 0) < iota((far_count, far_count), 1), 1.0, 0.0
    ).astype(BF16)
    rank = jnp.sum(mm(to_block_b, earlier) * to_block_f, 0, keepdims=True).astype(I32)
    values = jnp.concatenate(
        [far_cell[...].astype(F32), far_geom[0:6, :], jnp.zeros((1, far_count), F32)], 0
    )
    placed = [jnp.where(rank == r, values, 0.0) for r in range(CAP)]
    placed.append(jnp.zeros((2 * LANES - 8 * CAP, far_count), F32))
    request = exact(mm_nt, to_block_b, jnp.concatenate(placed, 0))
    lane = iota((VOL, 2 * LANES), 1)
    for s in range(GROUP):
        request = jnp.where(lane == 8 * CAP + s, ids[s].astype(F32), request)
    ask[:, 0, :] = request
    asked[pl.ds(me_vol, 1)] = ask[pl.ds(me_vol, 1)]

    sides = jnp.concatenate(
        [jnp.concatenate([adjacency[...], jnp.full((4, LANES - PATCHES), -1, I32)], 1)] * 2, 0
    ).astype(F32).T[0:PATCHES]
    patch_lane = iota((PATCHES, PATCHES), 1).astype(F32)
    facing = [jnp.where(patch_lane == sides[:, side:side + 1], 1.0, 0.0).astype(BF16) for side in range(4)]


    def take(cells, t, slot, bounded=False):
        for r in range(LANES):
            cell = jnp.clip(cells[t, r], 0, fields.shape[0] - 1) if bounded else cells[t, r]
            rows[slot, r:r + 1, :] = fields[pl.ds(cell, 1), :]
        return rows[slot].T

    def scatter(at, strength, s_param, t_param, patch):
        left[:, pl.ds(at, LANES)] = dot3(mm, sine_held[...], spline(s_param))
        weights = dot3(mm, sine[...], spline(t_param))
        if strength is not None:
            weights = weights * strength
        for s in range(GROUP):
            right[s * CTRL:(s + 1) * CTRL, pl.ds(at, LANES)] = jnp.where(patch == ids[s], weights, 0.0)

    def near_chunk(t, carry):
        at = pl.multiple_of(t * LANES, LANES)
        columns = take(near_cell, t, 0)
        geom = near_geom[:, pl.ds(at, LANES)]
        strength = densities(
            columns, [geom[i:i + 1] for i in range(3)], [geom[i:i + 1] for i in range(3, 6)]
        )
        scatter(at, strength, geom[6:7], geom[7:8], near_patch[:, pl.ds(at, LANES)])
        return carry

    load_fields.wait()
    for load in loads:
        load.wait()
    chunks = near_count // LANES
    lax.fori_loop(0, 11, near_chunk, 0)

    pl.semaphore_wait(barrier, VOL - 1 + DSG - 1)
    vol_start(0, ask, asked)
    lax.fori_loop(11, 14, near_chunk, 0)

    vol_wait(0, ask, asked)
    wanted = asked[:, 0, :].T
    tiles = []
    for t in range(CAP // 2):
        one = wanted[16 * t:16 * t + 8]
        two = wanted[16 * t + 8:16 * t + 16]
        tiles.append(jnp.concatenate([one, two], 1))
    cells_v[...] = jnp.concatenate(
        [jnp.clip((tile[0:1] + 0.5).astype(I32), 0, fields.shape[0] - 1) for tile in tiles] + [jnp.zeros((16 - CAP // 2, LANES), I32)], 0
    )
    to_scalar = pltpu.make_async_copy(cells_v, cells_s, local_sem)
    to_scalar.start()
    to_scalar.wait()
    dens[...] = jnp.zeros((LANES, LANES), F32)
    for t in range(CAP // 2):
        columns = take(cells_s, t, t % 4, True)
        tile = tiles[t]
        strength = densities(
            columns, [tile[i:i + 1] for i in range(1, 4)], [tile[i:i + 1] for i in range(4, 7)]
        )
        dens[2 * t:2 * t + 1, 0:VOL] = strength[:, 0:VOL]
        dens[2 * t + 1:2 * t + 2, 0:VOL] = strength[:, VOL:]
    reply[:, 0, :] = dens[...].T[0:VOL, :]
    replied[pl.ds(me_vol, 1)] = reply[pl.ds(me_vol, 1)]
    vol_start(1, reply, replied)

    lax.fori_loop(14, chunks, near_chunk, 0)
    near_grid = dot3(mm_nt, left[:, 0:near_count], right[:, 0:near_count])

    for t in range(far_count // LANES):
        at = slice(t * LANES, (t + 1) * LANES)
        scatter(near_count + t * LANES, None, far_geom[6:7, at], far_geom[7:8, at], far_patch[:, at])
    far_right, far_right_low = split2(right[:, near_count:])
    patch_of = iota((PATCHES, VOL), 0).astype(F32)
    places = [
        jnp.where(patch_of == wanted[8 * CAP + s:8 * CAP + s + 1, :], 1.0, 0.0).astype(BF16)
        for s in range(GROUP)
    ]
    vol_wait(1, reply, replied)
    answers = replied[:, 0, :].T
    high, middle, low = split3(answers)
    by_rank = mm(high, to_block_b) + mm(middle, to_block_b) + mm(low, to_block_b)
    far_strength = jnp.sum(
        jnp.where(iota((LANES, far_count), 0) == rank, by_rank, 0.0), 0, keepdims=True
    )
    far_out[...] = far_strength
    far_left, far_left_low = split2(left[:, near_count:] * far_strength)
    grid[:, 0, :] = (
        near_grid
        + mm_nt(far_left, far_right)
        + mm_nt(far_left, far_right_low)
        + mm_nt(far_left_low, far_right)
    )
    grids[pl.ds(me_vol, 1)] = grid[pl.ds(me_vol, 1)]
    vol_start(2, grid, grids)
    vol_wait(2, grid, grids)

    got = grids[:, 0, :]
    total = None
    for s in range(GROUP):
        term = picked(mm, places[s], got[:, s * CTRL:(s + 1) * CTRL])
        total = term if total is None else total + term
    for owner in range(DSG):
        base = owner * OWN
        for t in range(HALF):
            low = base + t // TILES * PIECE + t % TILES
            part[owner, :, t * LANES:t * LANES + CTRL] = total[low:low + 1]
            part[owner, :, t * LANES + CTRL:(t + 1) * LANES] = total[low + TILES:low + TILES + 1]
    parts[pl.ds(me_dsg, 1)] = part[pl.ds(me_dsg, 1)]
    dsg_start(0, lambda peer: part.at[peer], parts)
    dsg_wait(0, parts)
    summed = parts[0] + parts[1] + parts[2] + parts[3]
    me_core, me_chip = me_vol % VOL_C, me_vol // VOL_C
    for c in range(CHUNKS):
        line[c] = summed[:, c * SPAN:(c + 1) * SPAN]
        lines[c, me_core, me_chip] = line[c]
    for c in range(CHUNKS):

        def fan(t, carry, c=c):
            pltpu.make_async_remote_copy(
                src_ref=line.at[c],
                dst_ref=lines.at[c, me_core, me_chip],
                send_sem=row_send.at[c],
                recv_sem=row_recv.at[c],
                device_id={"vol": wrap(me_vol + VOL_C * t, VOL)},
                device_id_type=MESH,
            ).start()
            return carry

        lax.fori_loop(1, VOL // VOL_C, fan, 0)

    def hand_over(c):
        settle(lines.at[c, 0, pl.ds(0, VOL // VOL_C - 1)], row_recv.at[c])
        pltpu.make_async_remote_copy(
            src_ref=lines.at[c, me_core],
            dst_ref=lines.at[c, me_core],
            send_sem=core_send.at[c],
            recv_sem=core_recv.at[c],
            device_id={"vol": me_chip * VOL_C + 1 - me_core},
            device_id_type=MESH,
        ).start()

    span = []

    def edges_of(c):
        settle(lines.at[c, 0], core_recv.at[c])
        whole = lines[c].reshape(VOL, SPAN)
        tiles_here = [whole[:, t * LANES:(t + 1) * LANES] for t in range(TILES)]
        span.extend(tiles_here)
        across = dot3(mm, first[...], whole)
        across = jnp.concatenate(
            [across[:, t * LANES:(t + 1) * LANES] * lane_power[...] for t in range(TILES)], 0
        ).reshape(TILES, 8, LANES)
        along = jnp.concatenate(
            [dot3(mm_nt, pair_first[...], tile) * pair_power[...] for tile in tiles_here], 0
        ).reshape(TILES, 16, CTRL)
        row_sum = [None, None]
        col_sum = [[None, None], [None, None]]
        for n in range(3):
            for side in range(2):
                term = across[:, 2 * n + side, :]
                row_sum[side] = term if n == 0 else row_sum[side] + term
                at = n * 4 * CTRL + side * CTRL
                edges[c, 0:TILES, at:at + CTRL] = row_sum[side][:, 0:CTRL]
                edges[c, TILES:PIECE, at:at + CTRL] = row_sum[side][:, CTRL:]
                for half in range(2):
                    term = along[:, 6 * half + 2 * n + side, :]
                    col_sum[half][side] = term if n == 0 else col_sum[half][side] + term
                    at = n * 4 * CTRL + (2 + side) * CTRL
                    edges[c, half * TILES:(half + 1) * TILES, at:at + CTRL] = col_sum[half][side]
        all_edges[c, pl.ds(me_dsg, 1)] = edges[c][None]
        dsg_start(1 + c, lambda peer: edges.at[c], all_edges.at[c])

    hand_over(0)
    hand_over(1)
    edges_of(0)
    hand_over(2)
    edges_of(1)
    edges_of(2)
    for c in range(CHUNKS):
        settle(lines.at[c, 0, pl.ds(0, VOL // VOL_C - 1)], row_send.at[c])
        settle(lines.at[c, 0], core_send.at[c])

    halo_rows[...] = jnp.zeros((HALF, 8, LANES), F32)
    halo_cols[...] = jnp.zeros((HALF, 16, CTRL), F32)
    calm = dot3(mm, jnp.concatenate([tile * total_pair[...] for tile in span], 0), sine_pair[...])
    for t in range(HALF):
        design_out[t] = dot3(mm, sine[...], calm[t * CTRL:(t + 1) * CTRL])
    first_free = dot3(mm, first[...], sine[...])
    pair_first_free = dot3(mm, pair_first[...], sine_pair[...])
    for c in range(CHUNKS):
        dsg_wait(1 + c, all_edges.at[c])

    base = jnp.concatenate([all_edges[c, owner] for owner in range(DSG) for c in range(CHUNKS)], 0)

    def exchange(edge):
        taken = []
        for side in range(4):
            other = side ^ 1
            taken.append(picked(mm, facing[side], edge[:, other * CTRL:(other + 1) * CTRL]))
        return jnp.concatenate(taken, 1)

    width = 4 * CTRL
    halo0 = exchange(base[:, 0:width])
    halo1 = exchange(base[:, width:2 * width] + dot3(mm, halo0, spread0[...]))
    halo2 = exchange(
        base[:, 2 * width:] + dot3(mm, halo0, spread1[...]) + dot3(mm, halo1, spread0[...])
    )
    halo[0], halo[1], halo[2] = halo0, halo1, halo2
    mine = pl.ds(pl.multiple_of(me_dsg * OWN, 8), OWN)
    for k in range(3):
        own = halo[2 - k, mine, :]
        for side in range(2):
            row = 2 * k + side
            for c in range(CHUNKS):
                here = slice(c * TILES, (c + 1) * TILES)
                halves = [own[c * PIECE + half * TILES:c * PIECE + (half + 1) * TILES] for half in range(2)]
                at = side * CTRL
                pair = jnp.concatenate([half[:, at:at + CTRL] for half in halves], 1)
                halo_rows[here, row, :] = pair * (SMOOTHING * lane_power[row:row + 1, :])
                at = (2 + side) * CTRL
                for half in range(2):
                    halo_cols[here, 6 * half + row, :] = halves[half][:, at:at + CTRL] * (
                        SMOOTHING * pair_power[row:row + 1, :]
                    )
    rows_free = dot3(mm, halo_rows[...].reshape(HALF * 8, LANES), sine_pair[...])
    cols_free = dot3(mm, halo_cols[...].reshape(HALF * 16, CTRL), sine[...])
    for t in range(HALF):
        outer = jnp.concatenate([first_free, cols_free[t * 16:(t + 1) * 16]], 0)
        inner = jnp.concatenate([rows_free[t * 8:(t + 1) * 8], pair_first_free], 0)
        design_out[t] += dot3(mm_tn, outer, inner)


def finish(far_ref, pair_ref, far_out, design_out):
    far_out[...] = far_ref[...]
    for c in range(CHUNKS):
        for half in range(2):
            at = c * PIECE + half * TILES
            design_out[at:at + TILES] = pair_ref[
                c * TILES:(c + 1) * TILES, :, half * CTRL:(half + 1) * CTRL
            ]


def per_device(
    fields, far_geom, far_block, far_cell, far_patch, near_geom, near_cell, near_patch, adjacency
):
    far_count = far_cell.shape[0]
    near_count = near_cell.shape[0]
    points = far_count + near_count
    vmem = pl.BlockSpec(memory_space=pltpu.VMEM)
    smem = pl.BlockSpec(memory_space=pltpu.SMEM)
    stay = pl.BlockSpec(memory_space=pl.ANY)
    tables = [jnp.asarray(t) for t in constants()]
    dma = pltpu.SemaphoreType.DMA
    far, pairs = pl.pallas_call(
        kernel,
        out_shape=(
            jax.ShapeDtypeStruct((1, far_count), F32),
            jax.ShapeDtypeStruct((HALF, CTRL, LANES), F32),
        ),
        in_specs=[vmem] * 5 + [smem] + [vmem] * 2 + [stay] * (1 + len(tables)),
        out_specs=(vmem, vmem),
        scratch_shapes=[pltpu.VMEM(fields.shape, F32)]
        + [pltpu.VMEM(t.shape, F32) for t in tables]
        + [
            pltpu.VMEM((4, LANES, LANES), F32),
            pltpu.VMEM((CTRL, points), F32),
            pltpu.VMEM((GROUP * CTRL, points), F32),
            pltpu.VMEM((16, LANES), I32),
            pltpu.SMEM((16, LANES), I32),
            pltpu.VMEM((LANES, LANES), F32),
            pltpu.VMEM((VOL, 1, 2 * LANES), F32),
            pltpu.VMEM((VOL, 1, 2 * LANES), F32),
            pltpu.VMEM((VOL, 1, LANES), F32),
            pltpu.VMEM((VOL, 1, LANES), F32),
            pltpu.VMEM((VOL, 1, GROUP * CTRL), F32),
            pltpu.VMEM((VOL, 1, GROUP * CTRL), F32),
            pltpu.VMEM((DSG, 1, ROW), F32),
            pltpu.VMEM((DSG, 1, ROW), F32),
            pltpu.VMEM((CHUNKS, 1, SPAN), F32),
            pltpu.VMEM((CHUNKS, VOL_C, VOL // VOL_C, 1, SPAN), F32),
            pltpu.VMEM((CHUNKS, PIECE, 12 * CTRL), F32),
            pltpu.VMEM((CHUNKS, DSG, PIECE, 12 * CTRL), F32),
            pltpu.VMEM((3, PATCHES, 4 * CTRL), F32),
            pltpu.VMEM((HALF, 8, LANES), F32),
            pltpu.VMEM((HALF, 16, CTRL), F32),
            dma((3,)), dma((3,)), dma((1 + CHUNKS,)), dma((1 + CHUNKS,)),
            dma((CHUNKS,)), dma((CHUNKS,)), dma((CHUNKS,)), dma((CHUNKS,)),
            dma, dma((len(tables),)), dma,
        ],
        compiler_params=pltpu.CompilerParams(
            collective_id=0, has_side_effects=True, vmem_limit_bytes=60000 * 1024
        ),
    )(
        far_geom,
        far_block.reshape(1, far_count),
        far_cell.reshape(1, far_count),
        far_patch.reshape(1, far_count),
        near_geom,
        near_cell.reshape(near_count // LANES, LANES),
        near_patch.reshape(1, near_count),
        adjacency.T,
        fields,
        *tables,
    )
    far, design = pl.pallas_call(
        finish,
        out_shape=(
            jax.ShapeDtypeStruct((1, far_count), F32),
            jax.ShapeDtypeStruct((OWN, CTRL, CTRL), F32),
        ),
        in_specs=[vmem] * 2,
        out_specs=(vmem, vmem),
    )(far, pairs)
    return far.reshape(far_count), design


def solution(mesh):
    return jax.shard_map(
        per_device,
        mesh=mesh,
        in_specs=(
            P("vol", None),
            P(None, ("vol", "dsg")),
            P(("vol", "dsg"), None),
            P(("vol", "dsg")),
            P(("vol", "dsg")),
            P(None, ("vol", "dsg")),
            P(("vol", "dsg")),
            P(("vol", "dsg")),
            P(),
        ),
        out_specs=(P(("vol", "dsg")), P("dsg", None, None)),
        check_vma=False,
    )
```

```python
import jax
import jax.numpy as jnp
import numpy as np
from jax import lax
from jax.experimental import pallas as pl
from jax.experimental.pallas import tpu as pltpu
from jax.sharding import PartitionSpec as P

F32 = jnp.float32
BF16 = jnp.bfloat16
I32 = jnp.int32
MESH = pl.DeviceIdType.MESH

CTRL = 64
GROUP = 4
CAP = 20
PENALTY = 4.0
SMOOTHING = 16.0
LANES = 128
VOL = 64
VOL_C = 2
DSG = 4
PATCHES = 96
OWN = PATCHES // DSG
HALF = OWN // 2
CHUNKS = 3
TILES = HALF // CHUNKS
PIECE = OWN // CHUNKS
SPAN = TILES * LANES
ROW = OWN * CTRL
NOBODY = 999.0


def constants():
    order = np.arange(1, CTRL + 1)
    sine = np.sqrt(2.0 / (CTRL + 1)) * np.sin(np.pi * np.outer(order, order) / (CTRL + 1))
    spectrum = 2.0 - 2.0 * np.cos(np.pi * order / (CTRL + 1))
    inverse = 1.0 / (1.0 + SMOOTHING * spectrum)
    power = [inverse * (1.0 - inverse) ** k for k in range(4)]
    ends = [sine[0], sine[-1]]
    zero = np.zeros((CTRL, CTRL))
    sine_pair = np.block([[sine, zero], [zero, sine]])
    total = sum(np.outer(p, p) for p in power)
    total_pair = np.concatenate([total, total], 1)

    def spread(k):
        scale = SMOOTHING * np.outer(power[k], power[k])
        table = np.zeros((4, CTRL, 4, CTRL))
        for side in range(4):
            for at in range(CTRL):
                unit = np.zeros(CTRL)
                unit[at] = 1.0
                end = ends[side % 2]
                field = scale * (np.outer(end, unit) if side < 2 else np.outer(unit, end))
                table[side, at, 0] = ends[0] @ field
                table[side, at, 1] = ends[1] @ field
                table[side, at, 2] = field @ ends[0]
                table[side, at, 3] = field @ ends[1]
        return table.reshape(4 * CTRL, 4 * CTRL)

    first = np.zeros((8, CTRL))
    lane_power = np.zeros((8, LANES))
    pair_first = np.zeros((16, LANES))
    pair_power = np.zeros((16, CTRL))
    for k in range(3):
        for side in range(2):
            row = 2 * k + side
            first[row] = power[k] * ends[side]
            lane_power[row] = np.tile(power[k], 2)
            for half in range(2):
                pair_first[6 * half + row, half * CTRL:(half + 1) * CTRL] = power[k] * ends[side]
                pair_power[6 * half + row] = power[k]
    held = np.arange(VOL)
    held = held % VOL_C * (VOL // VOL_C) + held // VOL_C
    tables = (sine, sine[held], sine_pair, total_pair, spread(0), spread(1), first, lane_power, pair_first, pair_power)
    return [np.asarray(t, np.float32) for t in tables]


def iota(shape, axis):
    return lax.broadcasted_iota(I32, shape, axis)


def mm(a, b):
    return jnp.dot(a, b, preferred_element_type=F32)


def mm_nt(a, b):
    return lax.dot_general(a, b, (((1,), (1,)), ((), ())), preferred_element_type=F32)


def mm_tn(a, b):
    return lax.dot_general(a, b, (((0,), (0,)), ((), ())), preferred_element_type=F32)


def split2(x):
    high = x.astype(BF16)
    return high, (x - high.astype(F32)).astype(BF16)


def split3(x):
    high = x.astype(BF16)
    rest = x - high.astype(F32)
    middle = rest.astype(BF16)
    return high, middle, (rest - middle.astype(F32)).astype(BF16)


def exact(product, picks, x):
    high, middle, low = split3(x)
    picks = picks.astype(BF16)
    return product(picks, high) + product(picks, middle) + product(picks, low)


def picked(product, picks, x):
    high, low = split2(x)
    return product(picks, high) + product(picks, low)


def dot3(product, a, b):
    a_high, a_low = split2(a)
    b_high, b_low = split2(b)
    return product(a_high, b_high) + product(a_high, b_low) + product(a_low, b_high)


def bernstein(t):
    c = 1.0 - t
    values = [c * c * c, 3.0 * t * c * c, 3.0 * t * t * c, t * t * t]
    slopes = [-3.0 * c * c, 3.0 * c * c - 6.0 * t * c, 6.0 * t * c - 3.0 * t * t, 3.0 * t * t]
    return values, slopes


def pick(index, rows):
    return jnp.where(
        index == 0, rows[0], jnp.where(index == 1, rows[1], jnp.where(index == 2, rows[2], rows[3]))
    )


def densities(columns, coords, normals):
    count = columns.shape[1]
    value_x, slope_x = bernstein(coords[0])
    value_y, slope_y = bernstein(coords[1])
    value_z, slope_z = bernstein(coords[2])
    place = iota((16, count), 0)
    at_y, at_z = place // 4, place % 4
    value_y, slope_y = pick(at_y, value_y), pick(at_y, slope_y)
    value_z, slope_z = pick(at_z, value_z), pick(at_z, slope_z)
    plain, with_y, with_z = value_y * value_z, slope_y * value_z, value_y * slope_z
    point = []
    for base in (0, 64):
        parts = [columns[base + 16 * i:base + 16 * i + 16] for i in range(4)]
        value = parts[0] * value_x[0] + parts[1] * value_x[1] + parts[2] * value_x[2] + parts[3] * value_x[3]
        slope = parts[0] * slope_x[0] + parts[1] * slope_x[1] + parts[2] * slope_x[2] + parts[3] * slope_x[3]
        products = (value * plain, slope * plain, value * with_y, value * with_z)
        point.append([jnp.sum(product, 0, keepdims=True) for product in products])
    (u, ux, uy, uz), (w, wx, wy, wz) = point
    nx, ny, nz = normals
    squared = nx * nx + ny * ny + nz * nz
    inner = ux * wx + uy * wy + uz * wz
    along_u = ux * nx + uy * ny + uz * nz
    along_w = wx * nx + wy * ny + wz * nz
    return squared * inner - 2.0 * along_u * along_w + PENALTY * squared * u * w


def spline(param):
    scaled = param * (CTRL - 3.0)
    start = jnp.clip(jnp.floor(scaled), 0.0, CTRL - 4.0)
    x = scaled - start
    c = 1.0 - x
    square, cube = x * x, x * x * x
    weights = (
        c * c * c / 6.0,
        (3.0 * cube - 6.0 * square + 4.0) / 6.0,
        (-3.0 * cube + 3.0 * square + 3.0 * x + 1.0) / 6.0,
        cube / 6.0,
    )
    offset = iota((CTRL, param.shape[1]), 0) - start.astype(I32)
    result = jnp.where(offset == 3, weights[3], 0.0)
    for k in (2, 1, 0):
        result = jnp.where(offset == k, weights[k], result)
    return result


def kernel(
    far_geom, block, far_cell, far_patch, near_geom, near_cell, near_patch, adjacency,
    fields_in, sine_in, sine_held_in, sine_pair_in, total_pair_in, spread0_in, spread1_in, first_in, lane_power_in,
    pair_first_in, pair_power_in,
    far_out, design_out,
    fields, sine, sine_held, sine_pair, total_pair, spread0, spread1, first, lane_power, pair_first, pair_power,
    rows, left, right, cells_v, cells_s, dens, ask, asked, reply, replied, grid, grids, part, parts,
    line, lines, edges, all_edges, halo, halo_rows, halo_cols,
    vol_send, vol_recv, dsg_send, dsg_recv, row_send, row_recv, core_send, core_recv,
    local_sem, load_sem, fields_sem,
):
    me_vol = lax.axis_index("vol")
    me_dsg = lax.axis_index("dsg")
    far_count = far_geom.shape[1]
    near_count = near_geom.shape[1]

    load_fields = pltpu.make_async_copy(fields_in, fields, fields_sem)
    load_fields.start()
    loads = [
        pltpu.make_async_copy(source, target, load_sem.at[i])
        for i, (source, target) in enumerate(
            (
                (sine_in, sine), (sine_held_in, sine_held), (sine_pair_in, sine_pair), (total_pair_in, total_pair),
                (spread0_in, spread0), (spread1_in, spread1), (first_in, first),
                (lane_power_in, lane_power), (pair_first_in, pair_first), (pair_power_in, pair_power),
            )
        )
    ]
    for load in loads:
        load.start()

    barrier = pltpu.get_barrier_semaphore()

    def greet_vol(t, carry):
        peer = jnp.where(me_vol + t >= VOL, me_vol + t - VOL, me_vol + t)
        pl.semaphore_signal(barrier, inc=1, device_id={"vol": peer}, device_id_type=MESH)
        return carry

    lax.fori_loop(1, VOL, greet_vol, 0)
    for t in range(1, DSG):
        peer = jnp.where(me_dsg + t >= DSG, me_dsg + t - DSG, me_dsg + t)
        pl.semaphore_signal(barrier, inc=1, device_id={"dsg": peer}, device_id_type=MESH)

    def wrap(index, size):
        return jnp.where(index >= size, index - size, index)

    def vol_start(phase, source, target):
        def step(t, carry):
            peer = wrap(me_vol + t, VOL)
            pltpu.make_async_remote_copy(
                src_ref=source.at[peer],
                dst_ref=target.at[me_vol],
                send_sem=vol_send.at[phase],
                recv_sem=vol_recv.at[phase],
                device_id={"vol": peer},
                device_id_type=MESH,
            ).start()
            return carry

        lax.fori_loop(1, VOL, step, 0)

    def settle(ref, sem):
        pltpu.make_async_copy(ref, ref, sem).wait()

    def vol_wait(phase, source, target):
        settle(target.at[pl.ds(0, VOL - 1)], vol_recv.at[phase])
        settle(source.at[pl.ds(0, VOL - 1)], vol_send.at[phase])

    def dsg_start(phase, source, target):
        for t in (2, 1, 3):
            peer = wrap(me_dsg + t, DSG)
            pltpu.make_async_remote_copy(
                src_ref=source(peer),
                dst_ref=target.at[me_dsg],
                send_sem=dsg_send.at[phase],
                recv_sem=dsg_recv.at[phase],
                device_id={"dsg": peer},
                device_id_type=MESH,
            ).start()

    def dsg_wait(phase, target):
        settle(target.at[pl.ds(0, DSG - 1)], dsg_recv.at[phase])
        settle(target.at[pl.ds(0, DSG - 1)], dsg_send.at[phase])

    unseen = jnp.int32(PATCHES)
    near_ids, far_ids = near_patch[...], far_patch[...]
    ids = []
    previous = None
    for _ in range(GROUP):
        if previous is None:
            near_left, far_left = near_ids, far_ids
        else:
            near_left = jnp.where(near_ids > previous, near_ids, unseen)
            far_left = jnp.where(far_ids > previous, far_ids, unseen)
        previous = jnp.minimum(
            jnp.min(near_left, 1, keepdims=True), jnp.min(far_left, 1, keepdims=True)
        )
        ids.append(previous)

    to_block = iota((VOL, far_count), 0) == block[...]
    to_block_f = jnp.where(to_block, 1.0, 0.0)
    to_block_b = to_block_f.astype(BF16)
    earlier = jnp.where(
        iota((far_count, far_count), 0) < iota((far_count, far_count), 1), 1.0, 0.0
    ).astype(BF16)
    rank = jnp.sum(mm(to_block_b, earlier) * to_block_f, 0, keepdims=True).astype(I32)
    values = jnp.concatenate(
        [far_cell[...].astype(F32), far_geom[0:6, :], jnp.zeros((1, far_count), F32)], 0
    )
    placed = [jnp.where(rank == r, values, 0.0) for r in range(CAP)]
    placed.append(jnp.zeros((2 * LANES - 8 * CAP, far_count), F32))
    request = exact(mm_nt, to_block_b, jnp.concatenate(placed, 0))
    lane = iota((VOL, 2 * LANES), 1)
    for s in range(GROUP):
        request = jnp.where(lane == 8 * CAP + s, ids[s].astype(F32), request)
    ask[:, 0, :] = request
    asked[pl.ds(me_vol, 1)] = ask[pl.ds(me_vol, 1)]

    sides = jnp.concatenate(
        [jnp.concatenate([adjacency[...], jnp.full((4, LANES - PATCHES), -1, I32)], 1)] * 2, 0
    ).astype(F32).T[0:PATCHES]
    patch_lane = iota((PATCHES, PATCHES), 1).astype(F32)
    facing = [jnp.where(patch_lane == sides[:, side:side + 1], 1.0, 0.0).astype(BF16) for side in range(4)]


    def take(cells, t, slot):
        for r in range(LANES):
            rows[slot, r:r + 1, :] = fields[pl.ds(cells[t, r], 1), :]
        return rows[slot].T

    def scatter(at, strength, s_param, t_param, patch):
        left[:, pl.ds(at, LANES)] = dot3(mm, sine_held[...], spline(s_param))
        weights = dot3(mm, sine[...], spline(t_param))
        if strength is not None:
            weights = weights * strength
        for s in range(GROUP):
            right[s * CTRL:(s + 1) * CTRL, pl.ds(at, LANES)] = jnp.where(patch == ids[s], weights, 0.0)

    def near_chunk(t, carry):
        at = pl.multiple_of(t * LANES, LANES)
        columns = take(near_cell, t, 0)
        geom = near_geom[:, pl.ds(at, LANES)]
        strength = densities(
            columns, [geom[i:i + 1] for i in range(3)], [geom[i:i + 1] for i in range(3, 6)]
        )
        scatter(at, strength, geom[6:7], geom[7:8], near_patch[:, pl.ds(at, LANES)])
        return carry

    load_fields.wait()
    for load in loads:
        load.wait()
    chunks = near_count // LANES
    lax.fori_loop(0, 11, near_chunk, 0)

    pl.semaphore_wait(barrier, VOL - 1 + DSG - 1)
    vol_start(0, ask, asked)
    lax.fori_loop(11, 14, near_chunk, 0)

    vol_wait(0, ask, asked)
    wanted = asked[:, 0, :].T
    tiles = []
    for t in range(CAP // 2):
        one = wanted[16 * t:16 * t + 8]
        two = wanted[16 * t + 8:16 * t + 16]
        tiles.append(jnp.concatenate([one, two], 1))
    cells_v[...] = jnp.concatenate(
        [jnp.clip((tile[0:1] + 0.5).astype(I32), 0, fields.shape[0] - 1) for tile in tiles] + [jnp.zeros((16 - CAP // 2, LANES), I32)], 0
    )
    to_scalar = pltpu.make_async_copy(cells_v, cells_s, local_sem)
    to_scalar.start()
    to_scalar.wait()
    dens[...] = jnp.zeros((LANES, LANES), F32)
    for t in range(CAP // 2):
        columns = take(cells_s, t, t % 4)
        tile = tiles[t]
        strength = densities(
            columns, [tile[i:i + 1] for i in range(1, 4)], [tile[i:i + 1] for i in range(4, 7)]
        )
        dens[2 * t:2 * t + 1, 0:VOL] = strength[:, 0:VOL]
        dens[2 * t + 1:2 * t + 2, 0:VOL] = strength[:, VOL:]
    reply[:, 0, :] = dens[...].T[0:VOL, :]
    replied[pl.ds(me_vol, 1)] = reply[pl.ds(me_vol, 1)]
    vol_start(1, reply, replied)

    lax.fori_loop(14, chunks, near_chunk, 0)
    near_grid = dot3(mm_nt, left[:, 0:near_count], right[:, 0:near_count])

    for t in range(far_count // LANES):
        at = slice(t * LANES, (t + 1) * LANES)
        scatter(near_count + t * LANES, None, far_geom[6:7, at], far_geom[7:8, at], far_patch[:, at])
    far_right, far_right_low = split2(right[:, near_count:])
    patch_of = iota((PATCHES, VOL), 0).astype(F32)
    places = [
        jnp.where(patch_of == wanted[8 * CAP + s:8 * CAP + s + 1, :], 1.0, 0.0).astype(BF16)
        for s in range(GROUP)
    ]
    vol_wait(1, reply, replied)
    answers = replied[:, 0, :].T
    high, middle, low = split3(answers)
    by_rank = mm(high, to_block_b) + mm(middle, to_block_b) + mm(low, to_block_b)
    far_strength = jnp.sum(
        jnp.where(iota((LANES, far_count), 0) == rank, by_rank, 0.0), 0, keepdims=True
    )
    far_out[...] = far_strength
    far_left, far_left_low = split2(left[:, near_count:] * far_strength)
    grid[:, 0, :] = (
        near_grid
        + mm_nt(far_left, far_right)
        + mm_nt(far_left, far_right_low)
        + mm_nt(far_left_low, far_right)
    )
    grids[pl.ds(me_vol, 1)] = grid[pl.ds(me_vol, 1)]
    vol_start(2, grid, grids)
    vol_wait(2, grid, grids)

    got = grids[:, 0, :]
    total = None
    for s in range(GROUP):
        term = picked(mm, places[s], got[:, s * CTRL:(s + 1) * CTRL])
        total = term if total is None else total + term
    for owner in range(DSG):
        base = owner * OWN
        for c in range(CHUNKS):
            low = base + c * PIECE
            pair = jnp.concatenate([total[low:low + TILES], total[low + TILES:low + PIECE]], 1)
            for u in range(TILES):
                at = (c * TILES + u) * LANES
                part[owner, :, at:at + LANES] = pair[u:u + 1]
    parts[pl.ds(me_dsg, 1)] = part[pl.ds(me_dsg, 1)]
    dsg_start(0, lambda peer: part.at[peer], parts)
    dsg_wait(0, parts)
    summed = parts[0] + parts[1] + parts[2] + parts[3]
    me_core, me_chip = me_vol % VOL_C, me_vol // VOL_C
    for c in range(CHUNKS):
        line[c] = summed[:, c * SPAN:(c + 1) * SPAN]
        lines[c, me_core, me_chip] = line[c]
    for c in range(CHUNKS):

        def fan(t, carry, c=c):
            pltpu.make_async_remote_copy(
                src_ref=line.at[c],
                dst_ref=lines.at[c, me_core, me_chip],
                send_sem=row_send.at[c],
                recv_sem=row_recv.at[c],
                device_id={"vol": wrap(me_vol + VOL_C * t, VOL)},
                device_id_type=MESH,
            ).start()
            return carry

        lax.fori_loop(1, VOL // VOL_C, fan, 0)

    def hand_over(c):
        settle(lines.at[c, 0, pl.ds(0, VOL // VOL_C - 1)], row_recv.at[c])
        pltpu.make_async_remote_copy(
            src_ref=lines.at[c, me_core],
            dst_ref=lines.at[c, me_core],
            send_sem=core_send.at[c],
            recv_sem=core_recv.at[c],
            device_id={"vol": me_chip * VOL_C + 1 - me_core},
            device_id_type=MESH,
        ).start()

    span = []

    def edges_of(c):
        settle(lines.at[c, 0], core_recv.at[c])
        whole = lines[c].reshape(VOL, SPAN)
        tiles_here = [whole[:, t * LANES:(t + 1) * LANES] for t in range(TILES)]
        span.extend(tiles_here)
        across = dot3(mm, first[...], whole)
        across = jnp.concatenate(
            [across[:, t * LANES:(t + 1) * LANES] * lane_power[...] for t in range(TILES)], 0
        ).reshape(TILES, 8, LANES)
        along = jnp.concatenate(
            [dot3(mm_nt, pair_first[...], tile) * pair_power[...] for tile in tiles_here], 0
        ).reshape(TILES, 16, CTRL)
        row_sum = [None, None]
        col_sum = [[None, None], [None, None]]
        for n in range(3):
            for side in range(2):
                term = across[:, 2 * n + side, :]
                row_sum[side] = term if n == 0 else row_sum[side] + term
                at = n * 4 * CTRL + side * CTRL
                edges[c, 0:TILES, at:at + CTRL] = row_sum[side][:, 0:CTRL]
                edges[c, TILES:PIECE, at:at + CTRL] = row_sum[side][:, CTRL:]
                for half in range(2):
                    term = along[:, 6 * half + 2 * n + side, :]
                    col_sum[half][side] = term if n == 0 else col_sum[half][side] + term
                    at = n * 4 * CTRL + (2 + side) * CTRL
                    edges[c, half * TILES:(half + 1) * TILES, at:at + CTRL] = col_sum[half][side]
        all_edges[c, pl.ds(me_dsg, 1)] = edges[c][None]
        dsg_start(1 + c, lambda peer: edges.at[c], all_edges.at[c])

    hand_over(0)
    hand_over(1)
    edges_of(0)
    hand_over(2)
    edges_of(1)
    edges_of(2)
    for c in range(CHUNKS):
        settle(lines.at[c, 0, pl.ds(0, VOL // VOL_C - 1)], row_send.at[c])
        settle(lines.at[c, 0], core_send.at[c])

    halo_rows[...] = jnp.zeros((HALF, 8, LANES), F32)
    halo_cols[...] = jnp.zeros((HALF, 16, CTRL), F32)
    calm = dot3(mm, jnp.concatenate([tile * total_pair[...] for tile in span], 0), sine_pair[...])
    for t in range(HALF):
        design_out[t] = dot3(mm, sine[...], calm[t * CTRL:(t + 1) * CTRL])
    first_free = dot3(mm, first[...], sine[...])
    pair_first_free = dot3(mm, pair_first[...], sine_pair[...])
    for c in range(CHUNKS):
        dsg_wait(1 + c, all_edges.at[c])

    base = jnp.concatenate([all_edges[c, owner] for owner in range(DSG) for c in range(CHUNKS)], 0)

    def exchange(edge):
        taken = []
        for side in range(4):
            other = side ^ 1
            taken.append(picked(mm, facing[side], edge[:, other * CTRL:(other + 1) * CTRL]))
        return jnp.concatenate(taken, 1)

    width = 4 * CTRL
    halo0 = exchange(base[:, 0:width])
    halo1 = exchange(base[:, width:2 * width] + dot3(mm, halo0, spread0[...]))
    halo2 = exchange(
        base[:, 2 * width:] + dot3(mm, halo0, spread1[...]) + dot3(mm, halo1, spread0[...])
    )
    halo[0], halo[1], halo[2] = halo0, halo1, halo2
    mine = pl.ds(pl.multiple_of(me_dsg * OWN, 8), OWN)
    for k in range(3):
        own = halo[2 - k, mine, :]
        for side in range(2):
            row = 2 * k + side
            for c in range(CHUNKS):
                here = slice(c * TILES, (c + 1) * TILES)
                halves = [own[c * PIECE + half * TILES:c * PIECE + (half + 1) * TILES] for half in range(2)]
                at = side * CTRL
                pair = jnp.concatenate([half[:, at:at + CTRL] for half in halves], 1)
                halo_rows[here, row, :] = pair * (SMOOTHING * lane_power[row:row + 1, :])
                at = (2 + side) * CTRL
                for half in range(2):
                    halo_cols[here, 6 * half + row, :] = halves[half][:, at:at + CTRL] * (
                        SMOOTHING * pair_power[row:row + 1, :]
                    )
    rows_free = dot3(mm, halo_rows[...].reshape(HALF * 8, LANES), sine_pair[...])
    cols_free = dot3(mm, halo_cols[...].reshape(HALF * 16, CTRL), sine[...])
    for t in range(HALF):
        outer = jnp.concatenate([first_free, cols_free[t * 16:(t + 1) * 16]], 0)
        inner = jnp.concatenate([rows_free[t * 8:(t + 1) * 8], pair_first_free], 0)
        design_out[t] += dot3(mm_tn, outer, inner)


def finish(far_ref, pair_ref, far_out, design_out):
    far_out[...] = far_ref[...]
    for c in range(CHUNKS):
        for half in range(2):
            at = c * PIECE + half * TILES
            design_out[at:at + TILES] = pair_ref[
                c * TILES:(c + 1) * TILES, :, half * CTRL:(half + 1) * CTRL
            ]


def per_device(
    fields, far_geom, far_block, far_cell, far_patch, near_geom, near_cell, near_patch, adjacency
):
    far_count = far_cell.shape[0]
    near_count = near_cell.shape[0]
    points = far_count + near_count
    vmem = pl.BlockSpec(memory_space=pltpu.VMEM)
    smem = pl.BlockSpec(memory_space=pltpu.SMEM)
    stay = pl.BlockSpec(memory_space=pl.ANY)
    tables = [jnp.asarray(t) for t in constants()]
    dma = pltpu.SemaphoreType.DMA
    far, pairs = pl.pallas_call(
        kernel,
        out_shape=(
            jax.ShapeDtypeStruct((1, far_count), F32),
            jax.ShapeDtypeStruct((HALF, CTRL, LANES), F32),
        ),
        in_specs=[vmem] * 5 + [smem] + [vmem] * 2 + [stay] * (1 + len(tables)),
        out_specs=(vmem, vmem),
        scratch_shapes=[pltpu.VMEM(fields.shape, F32)]
        + [pltpu.VMEM(t.shape, F32) for t in tables]
        + [
            pltpu.VMEM((4, LANES, LANES), F32),
            pltpu.VMEM((CTRL, points), F32),
            pltpu.VMEM((GROUP * CTRL, points), F32),
            pltpu.VMEM((16, LANES), I32),
            pltpu.SMEM((16, LANES), I32),
            pltpu.VMEM((LANES, LANES), F32),
            pltpu.VMEM((VOL, 1, 2 * LANES), F32),
            pltpu.VMEM((VOL, 1, 2 * LANES), F32),
            pltpu.VMEM((VOL, 1, LANES), F32),
            pltpu.VMEM((VOL, 1, LANES), F32),
            pltpu.VMEM((VOL, 1, GROUP * CTRL), F32),
            pltpu.VMEM((VOL, 1, GROUP * CTRL), F32),
            pltpu.VMEM((DSG, 1, ROW), F32),
            pltpu.VMEM((DSG, 1, ROW), F32),
            pltpu.VMEM((CHUNKS, 1, SPAN), F32),
            pltpu.VMEM((CHUNKS, VOL_C, VOL // VOL_C, 1, SPAN), F32),
            pltpu.VMEM((CHUNKS, PIECE, 12 * CTRL), F32),
            pltpu.VMEM((CHUNKS, DSG, PIECE, 12 * CTRL), F32),
            pltpu.VMEM((3, PATCHES, 4 * CTRL), F32),
            pltpu.VMEM((HALF, 8, LANES), F32),
            pltpu.VMEM((HALF, 16, CTRL), F32),
            dma((3,)), dma((3,)), dma((1 + CHUNKS,)), dma((1 + CHUNKS,)),
            dma((CHUNKS,)), dma((CHUNKS,)), dma((CHUNKS,)), dma((CHUNKS,)),
            dma, dma((len(tables),)), dma,
        ],
        compiler_params=pltpu.CompilerParams(
            collective_id=0, has_side_effects=True, vmem_limit_bytes=60000 * 1024
        ),
    )(
        far_geom,
        far_block.reshape(1, far_count),
        far_cell.reshape(1, far_count),
        far_patch.reshape(1, far_count),
        near_geom,
        near_cell.reshape(near_count // LANES, LANES),
        near_patch.reshape(1, near_count),
        adjacency.T,
        fields,
        *tables,
    )
    far, design = pl.pallas_call(
        finish,
        out_shape=(
            jax.ShapeDtypeStruct((1, far_count), F32),
            jax.ShapeDtypeStruct((OWN, CTRL, CTRL), F32),
        ),
        in_specs=[vmem] * 2,
        out_specs=(vmem, vmem),
    )(far, pairs)
    return far.reshape(far_count), design


def solution(mesh):
    return jax.shard_map(
        per_device,
        mesh=mesh,
        in_specs=(
            P("vol", None),
            P(None, ("vol", "dsg")),
            P(("vol", "dsg"), None),
            P(("vol", "dsg")),
            P(("vol", "dsg")),
            P(None, ("vol", "dsg")),
            P(("vol", "dsg")),
            P(("vol", "dsg")),
            P(),
        ),
        out_specs=(P(("vol", "dsg")), P("dsg", None, None)),
        check_vma=False,
    )
```

```python
import jax
import jax.numpy as jnp
import numpy as np
from jax import lax
from jax.experimental import pallas as pl
from jax.experimental.pallas import tpu as pltpu
from jax.sharding import PartitionSpec as P

F32 = jnp.float32
BF16 = jnp.bfloat16
I32 = jnp.int32
MESH = pl.DeviceIdType.MESH

CTRL = 64
GROUP = 4
CAP = 20
PENALTY = 4.0
SMOOTHING = 16.0
LANES = 128
VOL = 64
VOL_C = 2
DSG = 4
PATCHES = 96
OWN = PATCHES // DSG
HALF = OWN // 2
CHUNKS = 3
TILES = HALF // CHUNKS
PIECE = OWN // CHUNKS
SPAN = TILES * LANES
ROW = OWN * CTRL
NOBODY = 999.0


def constants():
    order = np.arange(1, CTRL + 1)
    sine = np.sqrt(2.0 / (CTRL + 1)) * np.sin(np.pi * np.outer(order, order) / (CTRL + 1))
    spectrum = 2.0 - 2.0 * np.cos(np.pi * order / (CTRL + 1))
    inverse = 1.0 / (1.0 + SMOOTHING * spectrum)
    power = [inverse * (1.0 - inverse) ** k for k in range(4)]
    ends = [sine[0], sine[-1]]
    zero = np.zeros((CTRL, CTRL))
    sine_pair = np.block([[sine, zero], [zero, sine]])
    total = sum(np.outer(p, p) for p in power)
    total_pair = np.concatenate([total, total], 1)

    def spread(k):
        scale = SMOOTHING * np.outer(power[k], power[k])
        table = np.zeros((4, CTRL, 4, CTRL))
        for side in range(4):
            for at in range(CTRL):
                unit = np.zeros(CTRL)
                unit[at] = 1.0
                end = ends[side % 2]
                field = scale * (np.outer(end, unit) if side < 2 else np.outer(unit, end))
                table[side, at, 0] = ends[0] @ field
                table[side, at, 1] = ends[1] @ field
                table[side, at, 2] = field @ ends[0]
                table[side, at, 3] = field @ ends[1]
        return table.reshape(4 * CTRL, 4 * CTRL)

    first = np.zeros((8, CTRL))
    lane_power = np.zeros((8, LANES))
    pair_first = np.zeros((16, LANES))
    pair_power = np.zeros((16, CTRL))
    for k in range(3):
        for side in range(2):
            row = 2 * k + side
            first[row] = power[k] * ends[side]
            lane_power[row] = np.tile(power[k], 2)
            for half in range(2):
                pair_first[6 * half + row, half * CTRL:(half + 1) * CTRL] = power[k] * ends[side]
                pair_power[6 * half + row] = power[k]
    held = np.arange(VOL)
    held = held % VOL_C * (VOL // VOL_C) + held // VOL_C
    tables = (sine, sine[held], sine_pair, total_pair, spread(0), spread(1), first, lane_power, pair_first, pair_power)
    return [np.asarray(t, np.float32) for t in tables]


def iota(shape, axis):
    return lax.broadcasted_iota(I32, shape, axis)


def mm(a, b):
    return jnp.dot(a, b, preferred_element_type=F32)


def mm_nt(a, b):
    return lax.dot_general(a, b, (((1,), (1,)), ((), ())), preferred_element_type=F32)


def mm_tn(a, b):
    return lax.dot_general(a, b, (((0,), (0,)), ((), ())), preferred_element_type=F32)


def split2(x):
    high = x.astype(BF16)
    return high, (x - high.astype(F32)).astype(BF16)


def split3(x):
    high = x.astype(BF16)
    rest = x - high.astype(F32)
    middle = rest.astype(BF16)
    return high, middle, (rest - middle.astype(F32)).astype(BF16)


def exact(product, picks, x):
    high, middle, low = split3(x)
    picks = picks.astype(BF16)
    return product(picks, high) + product(picks, middle) + product(picks, low)


def picked(product, picks, x):
    high, low = split2(x)
    return product(picks, high) + product(picks, low)


def dot3(product, a, b):
    a_high, a_low = split2(a)
    b_high, b_low = split2(b)
    return product(a_high, b_high) + product(a_high, b_low) + product(a_low, b_high)


def bernstein(t):
    c = 1.0 - t
    values = [c * c * c, 3.0 * t * c * c, 3.0 * t * t * c, t * t * t]
    slopes = [-3.0 * c * c, 3.0 * c * c - 6.0 * t * c, 6.0 * t * c - 3.0 * t * t, 3.0 * t * t]
    return values, slopes


def pick(index, rows):
    return jnp.where(
        index == 0, rows[0], jnp.where(index == 1, rows[1], jnp.where(index == 2, rows[2], rows[3]))
    )


def densities(columns, coords, normals):
    count = columns.shape[1]
    value_x, slope_x = bernstein(coords[0])
    value_y, slope_y = bernstein(coords[1])
    value_z, slope_z = bernstein(coords[2])
    place = iota((16, count), 0)
    at_y, at_z = place // 4, place % 4
    value_y, slope_y = pick(at_y, value_y), pick(at_y, slope_y)
    value_z, slope_z = pick(at_z, value_z), pick(at_z, slope_z)
    plain, with_y, with_z = value_y * value_z, slope_y * value_z, value_y * slope_z
    point = []
    for base in (0, 64):
        parts = [columns[base + 16 * i:base + 16 * i + 16] for i in range(4)]
        value = parts[0] * value_x[0] + parts[1] * value_x[1] + parts[2] * value_x[2] + parts[3] * value_x[3]
        slope = parts[0] * slope_x[0] + parts[1] * slope_x[1] + parts[2] * slope_x[2] + parts[3] * slope_x[3]
        products = (value * plain, slope * plain, value * with_y, value * with_z)
        point.append([jnp.sum(product, 0, keepdims=True) for product in products])
    (u, ux, uy, uz), (w, wx, wy, wz) = point
    nx, ny, nz = normals
    squared = nx * nx + ny * ny + nz * nz
    inner = ux * wx + uy * wy + uz * wz
    along_u = ux * nx + uy * ny + uz * nz
    along_w = wx * nx + wy * ny + wz * nz
    return squared * inner - 2.0 * along_u * along_w + PENALTY * squared * u * w


def spline(param):
    scaled = param * (CTRL - 3.0)
    start = jnp.clip(jnp.floor(scaled), 0.0, CTRL - 4.0)
    x = scaled - start
    c = 1.0 - x
    square, cube = x * x, x * x * x
    weights = (
        c * c * c / 6.0,
        (3.0 * cube - 6.0 * square + 4.0) / 6.0,
        (-3.0 * cube + 3.0 * square + 3.0 * x + 1.0) / 6.0,
        cube / 6.0,
    )
    offset = iota((CTRL, param.shape[1]), 0) - start.astype(I32)
    result = jnp.where(offset == 3, weights[3], 0.0)
    for k in (2, 1, 0):
        result = jnp.where(offset == k, weights[k], result)
    return result


def kernel(
    far_geom, block, far_cell, far_patch, near_geom, near_cell, near_patch, adjacency,
    fields_in, sine_in, sine_held_in, sine_pair_in, total_pair_in, spread0_in, spread1_in, first_in, lane_power_in,
    pair_first_in, pair_power_in,
    far_out, design_out,
    fields, sine, sine_held, sine_pair, total_pair, spread0, spread1, first, lane_power, pair_first, pair_power,
    rows, left, right, cells_v, cells_s, dens, ask, asked, reply, replied, grid, grids, part, parts,
    line, lines, edges, all_edges, halo, halo_rows, halo_cols,
    vol_send, vol_recv, dsg_send, dsg_recv, row_send, row_recv, core_send, core_recv,
    local_sem, load_sem, fields_sem,
):
    me_vol = lax.axis_index("vol")
    me_dsg = lax.axis_index("dsg")
    far_count = far_geom.shape[1]
    near_count = near_geom.shape[1]

    load_fields = pltpu.make_async_copy(fields_in, fields, fields_sem)
    load_fields.start()
    loads = [
        pltpu.make_async_copy(source, target, load_sem.at[i])
        for i, (source, target) in enumerate(
            (
                (sine_in, sine), (sine_held_in, sine_held), (sine_pair_in, sine_pair), (total_pair_in, total_pair),
                (spread0_in, spread0), (spread1_in, spread1), (first_in, first),
                (lane_power_in, lane_power), (pair_first_in, pair_first), (pair_power_in, pair_power),
            )
        )
    ]
    for load in loads:
        load.start()

    barrier = pltpu.get_barrier_semaphore()

    def greet_vol(t, carry):
        peer = jnp.where(me_vol + t >= VOL, me_vol + t - VOL, me_vol + t)
        pl.semaphore_signal(barrier, inc=1, device_id={"vol": peer}, device_id_type=MESH)
        return carry

    lax.fori_loop(1, VOL, greet_vol, 0)
    for t in range(1, DSG):
        peer = jnp.where(me_dsg + t >= DSG, me_dsg + t - DSG, me_dsg + t)
        pl.semaphore_signal(barrier, inc=1, device_id={"dsg": peer}, device_id_type=MESH)

    def wrap(index, size):
        return jnp.where(index >= size, index - size, index)

    def vol_start(phase, source, target):
        def step(t, carry):
            peer = wrap(me_vol + t, VOL)
            pltpu.make_async_remote_copy(
                src_ref=source.at[peer],
                dst_ref=target.at[me_vol],
                send_sem=vol_send.at[phase],
                recv_sem=vol_recv.at[phase],
                device_id={"vol": peer},
                device_id_type=MESH,
            ).start()
            return carry

        lax.fori_loop(1, VOL, step, 0)

    def settle(ref, sem):
        pltpu.make_async_copy(ref, ref, sem).wait()

    def vol_wait(phase, source, target):
        settle(target.at[pl.ds(0, VOL - 1)], vol_recv.at[phase])
        settle(source.at[pl.ds(0, VOL - 1)], vol_send.at[phase])

    def dsg_start(phase, source, target):
        for t in (2, 1, 3):
            peer = wrap(me_dsg + t, DSG)
            pltpu.make_async_remote_copy(
                src_ref=source(peer),
                dst_ref=target.at[me_dsg],
                send_sem=dsg_send.at[phase],
                recv_sem=dsg_recv.at[phase],
                device_id={"dsg": peer},
                device_id_type=MESH,
            ).start()

    def dsg_wait(phase, target):
        settle(target.at[pl.ds(0, DSG - 1)], dsg_recv.at[phase])
        settle(target.at[pl.ds(0, DSG - 1)], dsg_send.at[phase])

    unseen = jnp.int32(PATCHES)
    near_ids, far_ids = near_patch[...], far_patch[...]
    ids = []
    previous = None
    for _ in range(GROUP):
        if previous is None:
            near_left, far_left = near_ids, far_ids
        else:
            near_left = jnp.where(near_ids > previous, near_ids, unseen)
            far_left = jnp.where(far_ids > previous, far_ids, unseen)
        previous = jnp.minimum(
            jnp.min(near_left, 1, keepdims=True), jnp.min(far_left, 1, keepdims=True)
        )
        ids.append(previous)

    to_block = iota((VOL, far_count), 0) == block[...]
    to_block_f = jnp.where(to_block, 1.0, 0.0)
    to_block_b = to_block_f.astype(BF16)
    earlier = jnp.where(
        iota((far_count, far_count), 0) < iota((far_count, far_count), 1), 1.0, 0.0
    ).astype(BF16)
    rank = jnp.sum(mm(to_block_b, earlier) * to_block_f, 0, keepdims=True).astype(I32)
    values = jnp.concatenate(
        [far_cell[...].astype(F32), far_geom[0:6, :], jnp.zeros((1, far_count), F32)], 0
    )
    placed = [jnp.where(rank == r, values, 0.0) for r in range(CAP)]
    placed.append(jnp.zeros((2 * LANES - 8 * CAP, far_count), F32))
    request = exact(mm_nt, to_block_b, jnp.concatenate(placed, 0))
    lane = iota((VOL, 2 * LANES), 1)
    for s in range(GROUP):
        request = jnp.where(lane == 8 * CAP + s, ids[s].astype(F32), request)
    ask[:, 0, :] = request
    asked[pl.ds(me_vol, 1)] = ask[pl.ds(me_vol, 1)]

    sides = jnp.concatenate(
        [jnp.concatenate([adjacency[...], jnp.full((4, LANES - PATCHES), -1, I32)], 1)] * 2, 0
    ).astype(F32).T[0:PATCHES]
    patch_lane = iota((PATCHES, PATCHES), 1).astype(F32)
    facing = [jnp.where(patch_lane == sides[:, side:side + 1], 1.0, 0.0).astype(BF16) for side in range(4)]


    def take(cells, t, slot):
        for r in range(LANES):
            rows[slot, r:r + 1, :] = fields[pl.ds(cells[t, r], 1), :]
        return rows[slot].T

    def scatter(at, strength, s_param, t_param, patch):
        left[:, pl.ds(at, LANES)] = dot3(mm, sine_held[...], spline(s_param))
        weights = dot3(mm, sine[...], spline(t_param))
        if strength is not None:
            weights = weights * strength
        for s in range(GROUP):
            right[s * CTRL:(s + 1) * CTRL, pl.ds(at, LANES)] = jnp.where(patch == ids[s], weights, 0.0)

    def near_chunk(t, carry):
        at = pl.multiple_of(t * LANES, LANES)
        columns = take(near_cell, t, 0)
        geom = near_geom[:, pl.ds(at, LANES)]
        strength = densities(
            columns, [geom[i:i + 1] for i in range(3)], [geom[i:i + 1] for i in range(3, 6)]
        )
        scatter(at, strength, geom[6:7], geom[7:8], near_patch[:, pl.ds(at, LANES)])
        return carry

    load_fields.wait()
    for load in loads:
        load.wait()
    chunks = near_count // LANES
    lax.fori_loop(0, 12, near_chunk, 0)

    pl.semaphore_wait(barrier, VOL - 1 + DSG - 1)
    vol_start(0, ask, asked)
    lax.fori_loop(12, chunks, near_chunk, 0)

    vol_wait(0, ask, asked)
    wanted = asked[:, 0, :].T
    tiles = []
    for t in range(CAP // 2):
        one = wanted[16 * t:16 * t + 8]
        two = wanted[16 * t + 8:16 * t + 16]
        tiles.append(jnp.concatenate([one, two], 1))
    cells_v[...] = jnp.concatenate(
        [jnp.clip((tile[0:1] + 0.5).astype(I32), 0, fields.shape[0] - 1) for tile in tiles] + [jnp.zeros((16 - CAP // 2, LANES), I32)], 0
    )
    to_scalar = pltpu.make_async_copy(cells_v, cells_s, local_sem)
    to_scalar.start()
    to_scalar.wait()
    dens[...] = jnp.zeros((LANES, LANES), F32)
    for t in range(CAP // 2):
        columns = take(cells_s, t, t % 4)
        tile = tiles[t]
        strength = densities(
            columns, [tile[i:i + 1] for i in range(1, 4)], [tile[i:i + 1] for i in range(4, 7)]
        )
        dens[2 * t:2 * t + 1, 0:VOL] = strength[:, 0:VOL]
        dens[2 * t + 1:2 * t + 2, 0:VOL] = strength[:, VOL:]
    reply[:, 0, :] = dens[...].T[0:VOL, :]
    replied[pl.ds(me_vol, 1)] = reply[pl.ds(me_vol, 1)]
    vol_start(1, reply, replied)

    near_grid = dot3(mm_nt, left[:, 0:near_count], right[:, 0:near_count])

    for t in range(far_count // LANES):
        at = slice(t * LANES, (t + 1) * LANES)
        scatter(near_count + t * LANES, None, far_geom[6:7, at], far_geom[7:8, at], far_patch[:, at])
    far_right, far_right_low = split2(right[:, near_count:])
    patch_of = iota((PATCHES, VOL), 0).astype(F32)
    places = [
        jnp.where(patch_of == wanted[8 * CAP + s:8 * CAP + s + 1, :], 1.0, 0.0).astype(BF16)
        for s in range(GROUP)
    ]
    vol_wait(1, reply, replied)
    answers = replied[:, 0, :].T
    high, middle, low = split3(answers)
    by_rank = mm(high, to_block_b) + mm(middle, to_block_b) + mm(low, to_block_b)
    far_strength = jnp.sum(
        jnp.where(iota((LANES, far_count), 0) == rank, by_rank, 0.0), 0, keepdims=True
    )
    far_out[...] = far_strength
    far_left, far_left_low = split2(left[:, near_count:] * far_strength)
    grid[:, 0, :] = (
        near_grid
        + mm_nt(far_left, far_right)
        + mm_nt(far_left, far_right_low)
        + mm_nt(far_left_low, far_right)
    )
    grids[pl.ds(me_vol, 1)] = grid[pl.ds(me_vol, 1)]
    vol_start(2, grid, grids)
    vol_wait(2, grid, grids)

    got = grids[:, 0, :]
    total = None
    for s in range(GROUP):
        term = picked(mm, places[s], got[:, s * CTRL:(s + 1) * CTRL])
        total = term if total is None else total + term
    for owner in range(DSG):
        base = owner * OWN
        for c in range(CHUNKS):
            low = base + c * PIECE
            pair = jnp.concatenate([total[low:low + TILES], total[low + TILES:low + PIECE]], 1)
            for u in range(TILES):
                at = (c * TILES + u) * LANES
                part[owner, :, at:at + LANES] = pair[u:u + 1]
    parts[pl.ds(me_dsg, 1)] = part[pl.ds(me_dsg, 1)]
    dsg_start(0, lambda peer: part.at[peer], parts)
    dsg_wait(0, parts)
    summed = parts[0] + parts[1] + parts[2] + parts[3]
    me_core, me_chip = me_vol % VOL_C, me_vol // VOL_C
    for c in range(CHUNKS):
        line[c] = summed[:, c * SPAN:(c + 1) * SPAN]
        lines[c, me_core, me_chip] = line[c]
    for c in range(CHUNKS):

        def fan(t, carry, c=c):
            pltpu.make_async_remote_copy(
                src_ref=line.at[c],
                dst_ref=lines.at[c, me_core, me_chip],
                send_sem=row_send.at[c],
                recv_sem=row_recv.at[c],
                device_id={"vol": wrap(me_vol + VOL_C * t, VOL)},
                device_id_type=MESH,
            ).start()
            return carry

        lax.fori_loop(1, VOL // VOL_C, fan, 0)

    def hand_over(c):
        settle(lines.at[c, 0, pl.ds(0, VOL // VOL_C - 1)], row_recv.at[c])
        pltpu.make_async_remote_copy(
            src_ref=lines.at[c, me_core],
            dst_ref=lines.at[c, me_core],
            send_sem=core_send.at[c],
            recv_sem=core_recv.at[c],
            device_id={"vol": me_chip * VOL_C + 1 - me_core},
            device_id_type=MESH,
        ).start()

    span = []

    def edges_of(c):
        settle(lines.at[c, 0], core_recv.at[c])
        whole = lines[c].reshape(VOL, SPAN)
        tiles_here = [whole[:, t * LANES:(t + 1) * LANES] for t in range(TILES)]
        span.extend(tiles_here)
        across = dot3(mm, first[...], whole)
        across = jnp.concatenate(
            [across[:, t * LANES:(t + 1) * LANES] * lane_power[...] for t in range(TILES)], 0
        ).reshape(TILES, 8, LANES)
        along = jnp.concatenate(
            [dot3(mm_nt, pair_first[...], tile) * pair_power[...] for tile in tiles_here], 0
        ).reshape(TILES, 16, CTRL)
        row_sum = [None, None]
        col_sum = [[None, None], [None, None]]
        for n in range(3):
            for side in range(2):
                term = across[:, 2 * n + side, :]
                row_sum[side] = term if n == 0 else row_sum[side] + term
                at = n * 4 * CTRL + side * CTRL
                edges[c, 0:TILES, at:at + CTRL] = row_sum[side][:, 0:CTRL]
                edges[c, TILES:PIECE, at:at + CTRL] = row_sum[side][:, CTRL:]
                for half in range(2):
                    term = along[:, 6 * half + 2 * n + side, :]
                    col_sum[half][side] = term if n == 0 else col_sum[half][side] + term
                    at = n * 4 * CTRL + (2 + side) * CTRL
                    edges[c, half * TILES:(half + 1) * TILES, at:at + CTRL] = col_sum[half][side]
        all_edges[c, pl.ds(me_dsg, 1)] = edges[c][None]
        dsg_start(1 + c, lambda peer: edges.at[c], all_edges.at[c])

    hand_over(0)
    hand_over(1)
    edges_of(0)
    hand_over(2)
    edges_of(1)
    edges_of(2)
    for c in range(CHUNKS):
        settle(lines.at[c, 0, pl.ds(0, VOL // VOL_C - 1)], row_send.at[c])
        settle(lines.at[c, 0], core_send.at[c])

    halo_rows[...] = jnp.zeros((HALF, 8, LANES), F32)
    halo_cols[...] = jnp.zeros((HALF, 16, CTRL), F32)
    calm = dot3(mm, jnp.concatenate([tile * total_pair[...] for tile in span], 0), sine_pair[...])
    for t in range(HALF):
        design_out[t] = dot3(mm, sine[...], calm[t * CTRL:(t + 1) * CTRL])
    first_free = dot3(mm, first[...], sine[...])
    pair_first_free = dot3(mm, pair_first[...], sine_pair[...])
    for c in range(CHUNKS):
        dsg_wait(1 + c, all_edges.at[c])

    base = jnp.concatenate([all_edges[c, owner] for owner in range(DSG) for c in range(CHUNKS)], 0)

    def exchange(edge):
        taken = []
        for side in range(4):
            other = side ^ 1
            taken.append(picked(mm, facing[side], edge[:, other * CTRL:(other + 1) * CTRL]))
        return jnp.concatenate(taken, 1)

    width = 4 * CTRL
    halo0 = exchange(base[:, 0:width])
    halo1 = exchange(base[:, width:2 * width] + dot3(mm, halo0, spread0[...]))
    halo2 = exchange(
        base[:, 2 * width:] + dot3(mm, halo0, spread1[...]) + dot3(mm, halo1, spread0[...])
    )
    halo[0], halo[1], halo[2] = halo0, halo1, halo2
    mine = pl.ds(pl.multiple_of(me_dsg * OWN, 8), OWN)
    for k in range(3):
        own = halo[2 - k, mine, :]
        for side in range(2):
            row = 2 * k + side
            for c in range(CHUNKS):
                here = slice(c * TILES, (c + 1) * TILES)
                halves = [own[c * PIECE + half * TILES:c * PIECE + (half + 1) * TILES] for half in range(2)]
                at = side * CTRL
                pair = jnp.concatenate([half[:, at:at + CTRL] for half in halves], 1)
                halo_rows[here, row, :] = pair * (SMOOTHING * lane_power[row:row + 1, :])
                at = (2 + side) * CTRL
                for half in range(2):
                    halo_cols[here, 6 * half + row, :] = halves[half][:, at:at + CTRL] * (
                        SMOOTHING * pair_power[row:row + 1, :]
                    )
    rows_free = dot3(mm, halo_rows[...].reshape(HALF * 8, LANES), sine_pair[...])
    cols_free = dot3(mm, halo_cols[...].reshape(HALF * 16, CTRL), sine[...])
    for t in range(HALF):
        outer = jnp.concatenate([first_free, cols_free[t * 16:(t + 1) * 16]], 0)
        inner = jnp.concatenate([rows_free[t * 8:(t + 1) * 8], pair_first_free], 0)
        design_out[t] += dot3(mm_tn, outer, inner)


def finish(far_ref, pair_ref, far_out, design_out):
    far_out[...] = far_ref[...]
    for c in range(CHUNKS):
        for half in range(2):
            at = c * PIECE + half * TILES
            design_out[at:at + TILES] = pair_ref[
                c * TILES:(c + 1) * TILES, :, half * CTRL:(half + 1) * CTRL
            ]


def per_device(
    fields, far_geom, far_block, far_cell, far_patch, near_geom, near_cell, near_patch, adjacency
):
    far_count = far_cell.shape[0]
    near_count = near_cell.shape[0]
    points = far_count + near_count
    vmem = pl.BlockSpec(memory_space=pltpu.VMEM)
    smem = pl.BlockSpec(memory_space=pltpu.SMEM)
    stay = pl.BlockSpec(memory_space=pl.ANY)
    tables = [jnp.asarray(t) for t in constants()]
    dma = pltpu.SemaphoreType.DMA
    far, pairs = pl.pallas_call(
        kernel,
        out_shape=(
            jax.ShapeDtypeStruct((1, far_count), F32),
            jax.ShapeDtypeStruct((HALF, CTRL, LANES), F32),
        ),
        in_specs=[vmem] * 5 + [smem] + [vmem] * 2 + [stay] * (1 + len(tables)),
        out_specs=(vmem, vmem),
        scratch_shapes=[pltpu.VMEM(fields.shape, F32)]
        + [pltpu.VMEM(t.shape, F32) for t in tables]
        + [
            pltpu.VMEM((4, LANES, LANES), F32),
            pltpu.VMEM((CTRL, points), F32),
            pltpu.VMEM((GROUP * CTRL, points), F32),
            pltpu.VMEM((16, LANES), I32),
            pltpu.SMEM((16, LANES), I32),
            pltpu.VMEM((LANES, LANES), F32),
            pltpu.VMEM((VOL, 1, 2 * LANES), F32),
            pltpu.VMEM((VOL, 1, 2 * LANES), F32),
            pltpu.VMEM((VOL, 1, LANES), F32),
            pltpu.VMEM((VOL, 1, LANES), F32),
            pltpu.VMEM((VOL, 1, GROUP * CTRL), F32),
            pltpu.VMEM((VOL, 1, GROUP * CTRL), F32),
            pltpu.VMEM((DSG, 1, ROW), F32),
            pltpu.VMEM((DSG, 1, ROW), F32),
            pltpu.VMEM((CHUNKS, 1, SPAN), F32),
            pltpu.VMEM((CHUNKS, VOL_C, VOL // VOL_C, 1, SPAN), F32),
            pltpu.VMEM((CHUNKS, PIECE, 12 * CTRL), F32),
            pltpu.VMEM((CHUNKS, DSG, PIECE, 12 * CTRL), F32),
            pltpu.VMEM((3, PATCHES, 4 * CTRL), F32),
            pltpu.VMEM((HALF, 8, LANES), F32),
            pltpu.VMEM((HALF, 16, CTRL), F32),
            dma((3,)), dma((3,)), dma((1 + CHUNKS,)), dma((1 + CHUNKS,)),
            dma((CHUNKS,)), dma((CHUNKS,)), dma((CHUNKS,)), dma((CHUNKS,)),
            dma, dma((len(tables),)), dma,
        ],
        compiler_params=pltpu.CompilerParams(
            collective_id=0, has_side_effects=True, vmem_limit_bytes=60000 * 1024
        ),
    )(
        far_geom,
        far_block.reshape(1, far_count),
        far_cell.reshape(1, far_count),
        far_patch.reshape(1, far_count),
        near_geom,
        near_cell.reshape(near_count // LANES, LANES),
        near_patch.reshape(1, near_count),
        adjacency.T,
        fields,
        *tables,
    )
    far, design = pl.pallas_call(
        finish,
        out_shape=(
            jax.ShapeDtypeStruct((1, far_count), F32),
            jax.ShapeDtypeStruct((OWN, CTRL, CTRL), F32),
        ),
        in_specs=[vmem] * 2,
        out_specs=(vmem, vmem),
    )(far, pairs)
    return far.reshape(far_count), design


def solution(mesh):
    return jax.shard_map(
        per_device,
        mesh=mesh,
        in_specs=(
            P("vol", None),
            P(None, ("vol", "dsg")),
            P(("vol", "dsg"), None),
            P(("vol", "dsg")),
            P(("vol", "dsg")),
            P(None, ("vol", "dsg")),
            P(("vol", "dsg")),
            P(("vol", "dsg")),
            P(),
        ),
        out_specs=(P(("vol", "dsg")), P("dsg", None, None)),
        check_vma=False,
    )
```
